512 devices in a mesh: row: 32 (over x, y), col: 16 (over z, core).
Axes of the slice: x: 4, y: 8, z: 8, core: 2. Of those that a mesh axis runs over, the one named last changes fastest.
Arguments:
- fine_blocks: bfloat16 [32, 16, 64, 128, 128], P('row', 'col'), may hold values from -0.5 to 0.5
- fine_rows: int32 [32, 16, 64], P('row', 'col'), may hold values from 0 to 7
- fine_cols: int32 [32, 16, 64], P('row', 'col'), may hold values from 0 to 39
- fine_counts: int32 [32, 16], P('row', 'col'), may hold values from 8 to 64, as said below
- prolong_blocks: bfloat16 [32, 16, 12, 128, 128], P('row', 'col'), may hold values from -1.5 to 1.5
- prolong_codes: int32 [32, 16, 12], P('row', 'col'), may hold values from 0 to 15, as said below
- prolong_counts: int32 [32, 16], P('row', 'col'), may hold values from 6 to 12, as said below
- second_blocks: bfloat16 [32, 16, 2, 128, 128], P('row', 'col'), may hold values from -0.25 to 0.25
- second_aggs: int32 [32, 16, 2], P('row', 'col'), may hold values from 0 to 1
Outputs:
- coarse_one: bfloat16 [32, 16, 2, 5, 2, 128, 128], P('row', 'col')
- coarse_two: float32 [32, 2, 3, 2, 128, 128], P('row')
The draws below stay inside these ranges and needn't reach their ends.
Inputs may be any that keep to these rules, and one draw needn't show every extreme that they name: Slots from fine_counts[r, c] to 63 are padding and are ignored; in every draw some device has all 64 slots live. `fine_cols`: a source outside the grid of devices contributes nothing. `prolong_codes`: the live slots of one device name distinct blocks. Slots from prolong_counts[r, c] to 11 are padding and are ignored; in every draw some device has all 12 slots live.
All inputs are finite; a program needn't handle non-finite values.
Results may differ from the reference program's by a relative error of at most 0.0057.
Values may be sent and summed in bfloat16 or wider, within the bound.
A program may use at most 64 MiB of HBM per device.

```python
import jax
import jax.numpy as jnp
from jax import lax

BS = 128
FB = 8
CB = 2
NA = 64
NP = 12
G2 = 2
NR = 32
NC = 16


def skewed_counts(key, lowest, highest, fullest):
    key_base, key_heavy, key_chosen = jax.random.split(key, 3)
    counts = jax.random.randint(key_base, (NR * NC,), lowest, highest + 1)
    heavy_rows = jax.random.randint(key_heavy, (NR * NC,), 0, 8) == 0
    counts = jnp.where(heavy_rows, fullest, counts)
    chosen = jax.random.randint(key_chosen, (), 0, NR * NC)
    counts = counts.at[chosen].set(fullest)
    return counts.reshape(NR, NC).astype(jnp.int32)


def draw_fine_counts(key, part):
    return skewed_counts(jax.random.fold_in(key, 11), NA // 8, NA // 2, NA)


def draw_prolong_counts(key, part):
    return skewed_counts(jax.random.fold_in(key, 23), NP // 2, NP, NP)


def draw_prolong_codes(key, part):
    device_keys = jax.random.split(jax.random.fold_in(key, 37), NR * NC)
    orders = jax.vmap(lambda one_key: jax.random.permutation(one_key, FB * CB))(device_keys)
    return orders[:, :NP].reshape(NR, NC, NP).astype(jnp.int32)


def with_ends(drawn, rng, smallest, high):
    longest = drawn.shape.index(max(drawn.shape))
    spots = []
    for shift in (0, 1):
        where = [jax.random.randint(jax.random.fold_in(rng, axis), (), 0, length) for axis, length in enumerate(drawn.shape)]
        where[longest] = (where[longest] + shift) % drawn.shape[longest]
        spots.append(tuple(where))
    return drawn.at[spots[0]].set(smallest).at[spots[1]].set(high)


def block_scale(key, extent, cuts, low, high):
    gain, own = 1.0, jax.random.fold_in(key, 6)
    for axis_at, shards_of in cuts:
        heights = jnp.exp(jax.random.uniform(jax.random.fold_in(own, axis_at), (shards_of,), jnp.float32, low / len(cuts), high / len(cuts)))
        gain = gain * jnp.repeat(heights, extent[axis_at] // shards_of).reshape([-1 if axis == axis_at else 1 for axis in range(len(extent))])
    return gain


def noise(stream_key, dims, scale, reach, cuts=(), kind=jnp.bfloat16):
    level = block_scale(stream_key, dims, cuts, -0.22, 0.18) if cuts else 1.0
    values = jax.random.normal(stream_key, dims, jnp.float32) * scale * level
    return jnp.minimum(jnp.maximum(values, -reach), reach).astype(kind)


def setup_inputs(seed: int = 0) -> dict:
    splits = jax.random.split(jax.random.key(seed), 10)
    fine_blocks = noise(splits[0], (NR, NC, NA, BS, BS), 0.09, 0.5, ((0, 32), (1, 16)))
    fine_rows = with_ends(jax.random.randint(splits[1], (NR, NC, NA), 0, FB), jax.random.fold_in(splits[1], 1), 0, FB - 1).astype(jnp.int32)
    fine_cols = with_ends(jax.random.randint(splits[2], (NR, NC, NA), 0, 5 * FB), jax.random.fold_in(splits[2], 1), 0, (5 * FB) - 1).astype(jnp.int32)
    fine_counts = draw_fine_counts(jax.random.fold_in(splits[9], 71), 0)
    prolong_blocks = noise(splits[4], (NR, NC, NP, BS, BS), 0.25, 1.5, ((0, 32), (1, 16)))
    prolong_codes = draw_prolong_codes(jax.random.fold_in(splits[9], 71), 0)
    prolong_counts = draw_prolong_counts(jax.random.fold_in(splits[9], 71), 0)
    second_blocks = noise(splits[7], (NR, NC, CB, BS, BS), 0.04, 0.25, ((0, 32), (1, 16)))
    second_aggs = with_ends(jax.random.randint(splits[8], (NR, NC, CB), 0, G2), jax.random.fold_in(splits[8], 1), 0, G2 - 1).astype(jnp.int32)
    return dict(fine_blocks=fine_blocks, fine_rows=fine_rows, fine_cols=fine_cols, fine_counts=fine_counts, prolong_blocks=prolong_blocks, prolong_codes=prolong_codes, prolong_counts=prolong_counts, second_blocks=second_blocks, second_aggs=second_aggs)


OFFSETS = ((0, 0), (0, -1), (0, 1), (-1, 0), (1, 0))
HIGHEST = lax.Precision.HIGHEST


def neighbour_blocks(table, row_at, col_at):
    gathered = []
    for row_step, col_step in OFFSETS:
        row_near = row_at + row_step
        col_near = col_at + col_step
        inside = (row_near >= 0) & (row_near < NR) & (col_near >= 0) & (col_near < NC)
        found = table[jnp.clip(row_near, 0, NR - 1), jnp.clip(col_near, 0, NC - 1)]
        gathered.append(jnp.where(inside, found, jnp.zeros_like(found)))
    return jnp.stack(gathered, axis=0)


def reference(fine_blocks, fine_rows, fine_cols, fine_counts, prolong_blocks, prolong_codes, prolong_counts, second_blocks, second_aggs):
    devices_flat = jnp.arange(NR * NC, dtype=jnp.int32)

    def dense_one(device_at):
        row_at = device_at // NC
        col_at = device_at % NC
        live_slots = jnp.arange(NP, dtype=jnp.int32) < prolong_counts[row_at, col_at]
        slot_codes = prolong_codes[row_at, col_at]
        placing = ((slot_codes[:, None] == jnp.arange(FB * CB, dtype=jnp.int32)[None, :]) & live_slots[:, None]).astype(jnp.float32)
        values = prolong_blocks[row_at, col_at].astype(jnp.float32)
        return jnp.einsum('kq,kxy->qxy', placing, values, precision=HIGHEST).astype(jnp.bfloat16)

    dense_all = lax.map(dense_one, devices_flat).reshape(NR, NC, FB * CB, BS, BS)

    def level_one(device_at):
        row_at = device_at // NC
        col_at = device_at % NC
        near_p = neighbour_blocks(dense_all, row_at, col_at).reshape(5 * FB, CB, BS, BS)
        columns = fine_cols[row_at, col_at]
        fetched = near_p[columns].astype(jnp.float32)
        blocks = fine_blocks[row_at, col_at].astype(jnp.float32)
        products = jnp.einsum('kxy,kjyz->kjxz', blocks, fetched, precision=HIGHEST)
        live_slots = jnp.arange(NA, dtype=jnp.int32) < fine_counts[row_at, col_at]
        products = jnp.where(live_slots[:, None, None, None], products, jnp.zeros_like(products))
        target = fine_rows[row_at, col_at] * 5 + columns // FB
        summed = jax.ops.segment_sum(products, target, num_segments=5 * FB)
        fine_product = lax.optimization_barrier(summed.astype(jnp.bfloat16)).astype(jnp.float32)
        fine_product = fine_product.reshape(FB, 5, CB, BS, BS)
        own_p = dense_all[row_at, col_at].reshape(FB, CB, BS, BS).astype(jnp.float32)
        result = jnp.einsum('iJxy,isjxz->Jsjyz', own_p, fine_product, precision=HIGHEST)
        return result.astype(jnp.bfloat16)

    coarse_one = lax.map(level_one, devices_flat).reshape(NR, NC, CB, 5, CB, BS, BS)

    member = (second_aggs[..., None] == jnp.arange(G2, dtype=jnp.int32)).astype(second_blocks.dtype)
    lifted_all = second_blocks[:, :, :, None] * member[..., None, None]

    def row_total(row_at):
        def one_device(col_at):
            near = neighbour_blocks(lifted_all, row_at, col_at).astype(jnp.float32)
            coarse = lax.optimization_barrier(coarse_one[row_at, col_at]).astype(jnp.float32)
            inside = jnp.einsum('Jsjxy,sjayz->Jaxz', coarse[:, 0:3], near[0:3], precision=HIGHEST)
            before = jnp.einsum('Jjxy,jayz->Jaxz', coarse[:, 3], near[3], precision=HIGHEST)
            beyond = jnp.einsum('Jjxy,jayz->Jaxz', coarse[:, 4], near[4], precision=HIGHEST)
            stacked = jnp.stack([inside, before, beyond], axis=1)
            half_prod = lax.optimization_barrier(stacked.astype(jnp.bfloat16)).astype(jnp.float32)
            own_lift = lifted_all[row_at, col_at].astype(jnp.float32)
            return jnp.einsum('Jaxy,Jgbxz->agbyz', own_lift, half_prod, precision=HIGHEST)

        terms = lax.map(one_device, jnp.arange(NC, dtype=jnp.int32))
        return jnp.sum(terms, axis=0)

    coarse_two = lax.map(row_total, jnp.arange(NR, dtype=jnp.int32))
    return coarse_one, coarse_two
```

```python
import jax
import jax.numpy as jnp
from jax import lax
from jax.experimental import pallas as pl
from jax.experimental.pallas import tpu as pltpu
from jax.sharding import PartitionSpec as P

BS = 128
FB = 8
CB = 2
NA = 64
NP = 12
G2 = 2
NR = 32
NC = 16
CHIPS = NC // 2
W2 = CB * BS
BF = jnp.bfloat16
F32 = jnp.float32
MESH = pl.DeviceIdType.MESH
HALF = (BS, 2 * BS)
REACH = (4, 3, 5, 2, 6, 1, 7)


def dot(a, b):
    return jnp.dot(a, b, preferred_element_type=F32)


def kernel(
    a_hbm,
    rows_hbm,
    cols_hbm,
    fcount_hbm,
    p_hbm,
    codes_hbm,
    pcount_hbm,
    l_hbm,
    aggs_hbm,
    one_ref,
    two_ref,
    a_buf,
    p_0,
    p_1,
    p_2,
    p_3,
    p_4,
    l_buf,
    rows_s,
    cols_v,
    fcount_v,
    codes_v,
    pcount_v,
    aggs_s,
    table_v,
    table_s,
    near_v,
    near_s,
    pt,
    run,
    wide,
    lifted,
    lifted_t,
    c1,
    give_e,
    give_l,
    take_e,
    take_l,
    part_e,
    part_l,
    rs_e,
    rs_l,
    all_e,
    all_l,
    load_sem,
    halo_send,
    halo_recv,
    pair_send,
    pair_recv,
    rs_send,
    rs_recv,
    ag_send,
    ag_recv,
    fw_send,
    fw_recv,
    reach_sem,
):
    p_bufs = (p_0, p_1, p_2, p_3, p_4)
    row = lax.axis_index("row")
    col = lax.axis_index("col")
    chip = col // 2
    core = col % 2
    partner = 2 * chip + 1 - core

    def at(dr, dc):
        return {"row": (row + dr + NR) % NR, "col": (col + dc + NC) % NC}

    sources = ((0, -1), (0, 1), (-1, 0), (1, 0))

    barrier = pltpu.get_barrier_semaphore()
    for dr, dc in sources:
        pl.semaphore_signal(barrier, inc=1, device_id=at(dr, dc), device_id_type=MESH)

    loads = [
        pltpu.make_async_copy(cols_hbm, cols_v, load_sem.at[0]),
        pltpu.make_async_copy(fcount_hbm, fcount_v, load_sem.at[1]),
        pltpu.make_async_copy(codes_hbm, codes_v.at[0], load_sem.at[2]),
        pltpu.make_async_copy(pcount_hbm, pcount_v.at[0], load_sem.at[3]),
        pltpu.make_async_copy(aggs_hbm, aggs_s.at[0], load_sem.at[4]),
        pltpu.make_async_copy(rows_hbm, rows_s, load_sem.at[5]),
        pltpu.make_async_copy(p_hbm, p_0.at[pl.ds(0, NP)], load_sem.at[6]),
        pltpu.make_async_copy(l_hbm, l_buf.at[0], load_sem.at[7]),
        pltpu.make_async_copy(a_hbm, a_buf, load_sem.at[8]),
    ]
    for load in loads:
        load.start()
    for s in range(5):
        p_bufs[s][NP] = jnp.zeros((BS, BS), BF)
    run[NA] = jnp.zeros((W2, BS), F32)

    pl.semaphore_wait(barrier, 4)

    def halo(s, item):
        src, dst = (
            (codes_hbm, codes_v.at[s]),
            (pcount_hbm, pcount_v.at[s]),
            (aggs_hbm, aggs_s.at[s]),
            (p_hbm, p_bufs[s].at[pl.ds(0, NP)]),
            (l_hbm, l_buf.at[s]),
        )[item]
        dr, dc = sources[s - 1]
        return pltpu.make_async_remote_copy(
            src_ref=src,
            dst_ref=dst,
            send_sem=halo_send.at[s - 1, item],
            recv_sem=halo_recv.at[s - 1, item],
            device_id=at(-dr, -dc),
            device_id_type=MESH,
        )

    order = (3, 4, 1, 2)
    for items in ((0, 1, 2), (3,), (4,)):
        for item in items:
            for s in order:
                halo(s, item).start()

    def widen(step, slot):
        sem = reach_sem.at[slot]
        for sign in (-1, 1):
            pl.semaphore_signal(sem, inc=1, device_id=at(0, sign * step), device_id_type=MESH)
        pl.semaphore_wait(sem, 2)

    for load in loads[:4]:
        load.wait()
    sub = lax.broadcasted_iota(jnp.int32, (BS, BS), 0)
    lane = lax.broadcasted_iota(jnp.int32, (BS, BS), 1)

    def down(vector, length):
        wide_row = jnp.broadcast_to(vector, (length, length))
        diag = sub[:length, :length] == lane[:length, :length]
        return jnp.max(jnp.where(diag, wide_row, -1), axis=1, keepdims=True)

    def pick(match, length, missing):
        best = jnp.max(jnp.where(match, sub[:length], -1), axis=0, keepdims=True)
        return jnp.where(best < 0, missing, best)

    cols = cols_v[...].reshape(1, NA)
    cols_down = down(cols, NA)
    live = sub[:NA] < fcount_v[...]
    cols_wide = jnp.concatenate([cols, cols], axis=1)
    table_v[0:1] = pick(
        (cols_down == cols_wide) & (sub[:NA] < lane[:NA]) & live, NA, NA
    )
    table_v[1:2] = pick((cols_down == lane[:NA]) & live, NA, NA)

    def place(s):
        codes = codes_v[s].reshape(1, NP)
        diag = sub[:16, :NP] == lane[:16, :NP]
        codes_down = jnp.max(
            jnp.where(diag, jnp.broadcast_to(codes, (16, NP)), -1), axis=1, keepdims=True
        )
        return pick((codes_down == lane[:16]) & (sub[:16] < pcount_v[s]), 16, NP)

    table_v[2:3] = place(0)
    send_table = pltpu.make_async_copy(table_v, table_s, load_sem.at[9])
    send_table.start()
    widen(1, 0)
    send_table.wait()
    loads[5].wait()
    loads[6].wait()

    def turn(i, carry):
        for coarse in range(CB):
            slot = table_s[2, i * CB + coarse]
            pt[i, pl.ds(coarse * BS, BS), :] = p_0[slot].T
        return carry

    lax.fori_loop(0, FB, turn, 0)
    loads[8].wait()

    def slots(step, carry):
        for inner in range(4):
            k = step * 4 + inner
            run[k] = dot(pt[rows_s[0, 0, k]], a_buf[k]) + run[table_s[0, k]]
        return carry

    lax.fori_loop(0, NA // 4, slots, 0)
    widen(2, 1)

    def widen_rows(s, carry):
        for m in range(FB):
            slot = table_s[1, s * FB + m]
            wide[s, m // 2, :, pl.ds((m % 2) * BS, BS)] = run[slot].astype(BF)
        return carry

    lax.fori_loop(0, 5, widen_rows, 0)
    widen(4, 2)

    for s in range(1, 5):
        for item in range(3):
            halo(s, item).wait_recv()
    for s in range(1, 5):
        near_v[s : s + 1] = place(s)
    near_v[0:1] = table_v[2:3]
    send_near = pltpu.make_async_copy(near_v, near_s, load_sem.at[10])
    send_near.start()
    loads[4].wait()
    loads[7].wait()

    def lift(s):
        for j in range(CB):
            block = l_buf[s, j]
            for a in range(G2):
                kept = jnp.where(aggs_s[s, 0, 0, j] == a, block, jnp.zeros_like(block))
                lifted[s, pl.ds(j * BS, BS), pl.ds(a * BS, BS)] = kept

    lift(0)
    lifted_t[...] = lifted[0].T
    send_near.wait()

    inside = (None, col > 0, col < NC - 1, row > 0, row < NR - 1)

    def level_one(s):
        total = jnp.zeros((W2, W2), F32)
        for pair in range(FB // 2):
            right = jnp.concatenate(
                [
                    jnp.concatenate(
                        [p_bufs[s][near_s[s, (2 * pair + low) * CB + j]] for j in range(CB)], axis=1
                    )
                    for low in range(2)
                ],
                axis=0,
            )
            total += dot(wide[s, pair], right)
        if inside[s] is not None:
            total = jnp.where(inside[s], total, jnp.zeros_like(total))
        result = total.astype(BF)
        for coarse in range(CB):
            for j in range(CB):
                one_ref[coarse, s, j] = result[
                    coarse * BS : (coarse + 1) * BS, j * BS : (j + 1) * BS
                ]
        return result

    def half_term(firsts):
        total = jnp.zeros((W2, W2), F32)
        for s, result in firsts:
            total += dot(result, lifted[s])
        return dot(lifted_t[...], total.astype(BF))

    gives, takes, parts = (give_e, give_l), (take_e, take_l), (part_e, part_l)
    shares, whole = (rs_e, rs_l), (all_e, all_l)

    def pair_copy(w):
        return pltpu.make_async_remote_copy(
            src_ref=gives[w].at[1 - core],
            dst_ref=takes[w],
            send_sem=pair_send.at[w],
            recv_sem=pair_recv.at[w],
            device_id={"row": row, "col": partner},
            device_id_type=MESH,
        )

    def peer(dz):
        return {"row": row, "col": 2 * ((chip + dz) % CHIPS) + core}

    def rs_copy(w, dz):
        return pltpu.make_async_remote_copy(
            src_ref=parts[w].at[(chip + dz) % CHIPS],
            dst_ref=shares[w].at[dz],
            send_sem=rs_send.at[w, dz],
            recv_sem=rs_recv.at[w, dz],
            device_id=peer(dz),
            device_id_type=MESH,
        )

    def ag_copy(w, dz):
        return pltpu.make_async_remote_copy(
            src_ref=whole[w].at[core, chip],
            dst_ref=whole[w].at[core, chip],
            send_sem=ag_send.at[w, dz],
            recv_sem=ag_recv.at[w, dz],
            device_id=peer(dz),
            device_id_type=MESH,
        )

    def ag_arrival(w, dz):
        landing = whole[w].at[core, (chip - dz + CHIPS) % CHIPS]
        return pltpu.make_async_remote_copy(
            src_ref=landing,
            dst_ref=landing,
            send_sem=ag_send.at[w, dz],
            recv_sem=ag_recv.at[w, dz],
            device_id=peer(dz),
            device_id_type=MESH,
        )

    def forward(w, dz):
        piece = whole[w].at[core, (chip - dz + CHIPS) % CHIPS]
        return pltpu.make_async_remote_copy(
            src_ref=piece,
            dst_ref=piece,
            send_sem=fw_send.at[w, dz],
            recv_sem=fw_recv.at[w, dz],
            device_id={"row": row, "col": partner},
            device_id_type=MESH,
        )

    def forward_arrival(w, dz):
        piece = whole[w].at[1 - core, (chip - dz + CHIPS) % CHIPS]
        return pltpu.make_async_remote_copy(
            src_ref=piece,
            dst_ref=piece,
            send_sem=fw_send.at[w, dz],
            recv_sem=fw_recv.at[w, dz],
            device_id={"row": row, "col": partner},
            device_id_type=MESH,
        )

    def scatter(w):
        pair_copy(w).wait_recv()
        total = gives[w][core].astype(F32) + takes[w][...].astype(F32)
        parts[w][...] = total.astype(BF).reshape(CHIPS, HALF[w] // CHIPS, W2)
        for dz in REACH:
            rs_copy(w, dz).start()

    def gather(w):
        total = parts[w][chip].astype(F32)
        for dz in REACH[::-1]:
            rs_copy(w, dz).wait_recv()
            total += shares[w][dz].astype(F32)
        whole[w][core, chip] = total.astype(BF)
        for dz in REACH:
            ag_copy(w, dz).start()
        forward(w, 0).start()

    def hand_over(w):
        for dz in REACH[::-1]:
            ag_arrival(w, dz).wait_recv()
            forward(w, dz).start()

    firsts = [(0, level_one(0))]
    for s in (1, 2):
        halo(s, 3).wait_recv()
        firsts.append((s, level_one(s)))
    for s in (1, 2):
        halo(s, 4).wait_recv()
        lift(s)
    early = half_term(firsts).astype(BF)
    for side in range(2):
        give_e[side] = early[side * BS : (side + 1) * BS]
    pair_copy(0).start()
    scatter(0)

    for s in (3, 4):
        halo(s, 3).wait_recv()
        result = level_one(s)
        halo(s, 4).wait_recv()
        lift(s)
        give_l[s - 3] = half_term([(s, result)]).astype(BF)
    pair_copy(1).start()
    gather(0)
    scatter(1)
    hand_over(0)
    gather(1)
    hand_over(1)
    for w in range(2):
        for dz in range(CHIPS):
            forward_arrival(w, dz).wait_recv()
        size = HALF[w] // CHIPS
        for side in range(2):
            for piece in range(CHIPS):
                block = whole[w][side, piece].astype(F32)
                if w == 0:
                    a, g, y = side, 0, piece * size
                else:
                    a, g, y = piece // 4, 1 + side, (piece % 4) * size
                for b in range(G2):
                    two_ref[a, g, b, pl.ds(y, size), :] = block[:, b * BS : (b + 1) * BS]

    for s in range(1, 5):
        for item in range(5):
            halo(s, item).wait_send()
    for w in range(2):
        pair_copy(w).wait_send()
        for dz in REACH:
            rs_copy(w, dz).wait_send()
            ag_copy(w, dz).wait_send()
        for dz in range(CHIPS):
            forward(w, dz).wait_send()


def per_device(
    fine_blocks,
    fine_rows,
    fine_cols,
    fine_counts,
    prolong_blocks,
    prolong_codes,
    prolong_counts,
    second_blocks,
    second_aggs,
):
    any_spec = pl.BlockSpec(memory_space=pl.ANY)
    vmem = pl.BlockSpec(memory_space=pltpu.VMEM)
    dma = pltpu.SemaphoreType.DMA
    one, two = pl.pallas_call(
        kernel,
        name="galerkin",
        out_shape=(
            jax.ShapeDtypeStruct((CB, 5, CB, BS, BS), BF),
            jax.ShapeDtypeStruct((G2, 3, G2, BS, BS), F32),
        ),
        in_specs=[any_spec] * 9,
        out_specs=(vmem, vmem),
        scratch_shapes=[
            pltpu.VMEM((NA, BS, BS), BF),
            *[pltpu.VMEM((NP + 1, BS, BS), BF)] * 5,
            pltpu.VMEM((5, CB, BS, BS), BF),
            pltpu.SMEM((1, 1, NA), jnp.int32),
            pltpu.VMEM((1, 1, NA), jnp.int32),
            pltpu.VMEM((1, 1), jnp.int32),
            pltpu.VMEM((5, 1, 1, NP), jnp.int32),
            pltpu.VMEM((5, 1, 1), jnp.int32),
            pltpu.SMEM((5, 1, 1, CB), jnp.int32),
            pltpu.VMEM((8, BS), jnp.int32),
            pltpu.SMEM((8, BS), jnp.int32),
            pltpu.VMEM((8, BS), jnp.int32),
            pltpu.SMEM((8, BS), jnp.int32),
            pltpu.VMEM((FB, W2, BS), BF),
            pltpu.VMEM((NA + 1, W2, BS), F32),
            pltpu.VMEM((5, FB // 2, W2, W2), BF),
            pltpu.VMEM((5, W2, W2), BF),
            pltpu.VMEM((W2, W2), BF),
            pltpu.VMEM((8, BS), BF),
            pltpu.VMEM((2, HALF[0], W2), BF),
            pltpu.VMEM((2, HALF[1], W2), BF),
            pltpu.VMEM((HALF[0], W2), BF),
            pltpu.VMEM((HALF[1], W2), BF),
            pltpu.VMEM((CHIPS, HALF[0] // CHIPS, W2), BF),
            pltpu.VMEM((CHIPS, HALF[1] // CHIPS, W2), BF),
            pltpu.VMEM((CHIPS, HALF[0] // CHIPS, W2), BF),
            pltpu.VMEM((CHIPS, HALF[1] // CHIPS, W2), BF),
            pltpu.VMEM((2, CHIPS, HALF[0] // CHIPS, W2), BF),
            pltpu.VMEM((2, CHIPS, HALF[1] // CHIPS, W2), BF),
            dma((11,)),
            dma((4, 5)),
            dma((4, 5)),
            dma((2,)),
            dma((2,)),
            dma((2, CHIPS)),
            dma((2, CHIPS)),
            dma((2, CHIPS)),
            dma((2, CHIPS)),
            dma((2, CHIPS)),
            dma((2, CHIPS)),
            pltpu.SemaphoreType.REGULAR((3,)),
        ],
        compiler_params=pltpu.CompilerParams(
            collective_id=0, has_side_effects=True, vmem_limit_bytes=48 << 20
        ),
    )(
        fine_blocks[0, 0],
        fine_rows,
        fine_cols,
        fine_counts,
        prolong_blocks[0, 0],
        prolong_codes,
        prolong_counts,
        second_blocks[0, 0],
        second_aggs,
    )
    return (one[None, None], two[None])


def solution(mesh):
    in_specs = (
        P("row", "col", None, None, None),
        P("row", "col", None),
        P("row", "col", None),
        P("row", "col"),
        P("row", "col", None, None, None),
        P("row", "col", None),
        P("row", "col"),
        P("row", "col", None, None, None),
        P("row", "col", None),
    )
    out_specs = (
        P("row", "col", None, None, None, None, None),
        P("row", None, None, None, None, None),
    )
    return jax.shard_map(
        per_device, mesh=mesh, in_specs=in_specs, out_specs=out_specs, check_vma=False
    )
```

```python
import jax
import jax.numpy as jnp
from jax import lax
from jax.experimental import pallas as pl
from jax.experimental.pallas import tpu as pltpu
from jax.sharding import PartitionSpec as P

BS = 128
FB = 8
CB = 2
NA = 64
NP = 12
G2 = 2
NR = 32
NC = 16
CHIPS = NC // 2
W2 = CB * BS
BF = jnp.bfloat16
F32 = jnp.float32
MESH = pl.DeviceIdType.MESH
VMEM_LIMIT = 62 << 20
HALF = (BS, 2 * BS)
REACH = (4, 3, 5, 2, 6, 1, 7)


def dot(a, b):
    return jnp.dot(a, b, preferred_element_type=F32)


def kernel(
    meta_hbm,
    a_hbm,
    p_hbm,
    l_hbm,
    one_hbm,
    early_hbm,
    late_hbm,
    a_buf,
    p_0,
    p_1,
    p_2,
    p_3,
    p_4,
    l_buf,
    meta_v,
    meta_s,
    table_v,
    table_s,
    near_v,
    near_s,
    pt,
    run,
    one_ref,
    wide,
    lifted,
    lifted_t,
    give_e,
    give_l,
    take_e,
    take_l,
    part_e,
    part_l,
    rs_e,
    rs_l,
    all_e,
    all_l,
    load_sem,
    halo_send,
    halo_recv,
    pair_send,
    pair_recv,
    rs_send,
    rs_recv,
    ag_send,
    ag_recv,
    fw_send,
    fw_recv,
    store_sem,
    reach_sem,
):
    p_bufs = (p_0, p_1, p_2, p_3, p_4)
    row = lax.axis_index("row")
    col = lax.axis_index("col")
    chip = col // 2
    core = col % 2
    partner = 2 * chip + 1 - core

    def at(dr, dc):
        return {"row": (row + dr + NR) % NR, "col": (col + dc + NC) % NC}

    sources = ((0, -1), (0, 1), (-1, 0), (1, 0))

    has = (None, col > 0, col < NC - 1, row > 0, row < NR - 1)
    feeds = (None, has[2], has[1], has[4], has[3])

    barrier = pltpu.get_barrier_semaphore()
    for (dr, dc), near in zip(sources, has[1:]):

        @pl.when(near)
        def _():
            pl.semaphore_signal(barrier, inc=1, device_id=at(dr, dc), device_id_type=MESH)


    loads = [
        pltpu.make_async_copy(meta_hbm, meta_v.at[0], load_sem.at[0]),
        pltpu.make_async_copy(meta_hbm, meta_s, load_sem.at[1]),
        pltpu.make_async_copy(p_hbm, p_0.at[pl.ds(0, NP)], load_sem.at[2]),
        pltpu.make_async_copy(l_hbm, l_buf.at[0], load_sem.at[3]),
        pltpu.make_async_copy(a_hbm, a_buf, load_sem.at[4]),
    ]
    for load in loads:
        load.start()
    for s in range(5):
        p_bufs[s][NP] = jnp.zeros((BS, BS), BF)
    run[NA] = jnp.zeros((W2, BS), F32)

    for s in range(1, 5):

        @pl.when(jnp.logical_not(has[s]))
        def _():
            meta_v[s] = jnp.zeros((8, BS), jnp.int32)
            l_buf[s] = jnp.zeros((CB, BS, BS), BF)

    pl.semaphore_wait(barrier, sum(near.astype(jnp.int32) for near in has[1:]))

    def halo(s, item):
        src, dst = (
            (meta_hbm, meta_v.at[s]),
            (p_hbm, p_bufs[s].at[pl.ds(0, NP)]),
            (l_hbm, l_buf.at[s]),
        )[item]
        dr, dc = sources[s - 1]
        return pltpu.make_async_remote_copy(
            src_ref=src,
            dst_ref=dst,
            send_sem=halo_send.at[s - 1, item],
            recv_sem=halo_recv.at[s - 1, item],
            device_id=at(-dr, -dc),
            device_id_type=MESH,
        )

    order = (3, 4, 1, 2)
    for item in range(3):
        for s in order:

            @pl.when(feeds[s])
            def _():
                halo(s, item).start()

    def arrived(s, item):
        @pl.when(has[s])
        def _():
            halo(s, item).wait_recv()


    def spread(step, slot):
        for sign in (-1, 1):

            @pl.when((col + sign * step >= 0) & (col + sign * step < NC))
            def _():
                pl.semaphore_signal(
                    reach_sem.at[slot], inc=1, device_id=at(0, sign * step), device_id_type=MESH
                )

    def known(step, slot):
        ends = (col >= step).astype(jnp.int32) + (col < NC - step).astype(jnp.int32)
        pl.semaphore_wait(reach_sem.at[slot], ends)

    spread(1, 0)

    loads[0].wait()
    sub = lax.broadcasted_iota(jnp.int32, (BS, BS), 0)
    lane = lax.broadcasted_iota(jnp.int32, (BS, BS), 1)

    def down(vector, length):
        diag = sub[:length] == lane[:length]
        return jnp.max(jnp.where(diag, vector, -1), axis=1, keepdims=True)

    def pick(match, length, missing):
        best = jnp.max(jnp.where(match, sub[:length], -1), axis=0, keepdims=True)
        return jnp.where(best < 0, missing, best)

    cols = meta_v[0, 0:1]
    cols_down = down(cols, NA)
    live = sub[:NA] < meta_v[0, 2:3]
    table_v[0:1] = pick((cols_down == cols) & (sub[:NA] < lane[:NA]) & live, NA, NA)
    table_v[1:2] = pick((cols_down == lane[:NA]) & live, NA, NA)

    def place(s):
        codes_down = down(meta_v[s, 3:4], 16)
        return pick((codes_down == lane[:16]) & (sub[:16] < meta_v[s, 4:5]), 16, NP)

    table_v[2:3] = place(0)
    send_table = pltpu.make_async_copy(table_v, table_s, load_sem.at[5])
    send_table.start()
    send_table.wait()
    loads[1].wait()
    loads[2].wait()

    def turn(i, carry):
        for coarse in range(CB):
            slot = table_s[2, i * CB + coarse]
            pt[i, pl.ds(coarse * BS, BS), :] = p_0[slot].T
        return carry

    lax.fori_loop(0, FB, turn, 0)
    known(1, 0)
    spread(2, 1)
    loads[4].wait()

    def slots(step, carry):
        for inner in range(4):
            k = step * 4 + inner
            run[k] = dot(pt[meta_s[1, k]], a_buf[k]) + run[table_s[0, k]]
        return carry

    lax.fori_loop(0, NA // 4, slots, 0)
    known(2, 1)
    spread(4, 2)

    def widen_rows(s, carry):
        for m in range(FB):
            slot = table_s[1, s * FB + m]
            wide[s, m // 2, :, pl.ds((m % 2) * BS, BS)] = run[slot].astype(BF)
        return carry

    lax.fori_loop(0, 5, widen_rows, 0)
    known(4, 2)
    spread(8, 3)

    for s in range(1, 5):
        arrived(s, 0)
    near_v[0:1] = table_v[2:3]
    near_v[8:9] = meta_v[0, 5:6]
    for s in range(1, 5):
        near_v[s : s + 1] = place(s)
        near_v[8 + s : 9 + s] = meta_v[s, 5:6]
    send_near = pltpu.make_async_copy(near_v, near_s, load_sem.at[6])
    send_near.start()
    loads[3].wait()

    def lift(s):
        for j in range(CB):
            block = l_buf[s, j]
            for a in range(G2):
                kept = jnp.where(near_s[8 + s, j] == a, block, jnp.zeros_like(block))
                lifted[s, pl.ds(j * BS, BS), pl.ds(a * BS, BS)] = kept

    send_near.wait()
    lift(0)
    lifted_t[...] = lifted[0].T

    def level_one(s):
        total = jnp.zeros((W2, W2), F32)
        for pair in range(FB // 2):
            right = jnp.concatenate(
                [
                    jnp.concatenate(
                        [p_bufs[s][near_s[s, (2 * pair + low) * CB + j]] for j in range(CB)], axis=1
                    )
                    for low in range(2)
                ],
                axis=0,
            )
            total += dot(wide[s, pair], right)
        result = total.astype(BF)
        for coarse in range(CB):
            for j in range(CB):
                one_ref[coarse, s, j] = result[
                    coarse * BS : (coarse + 1) * BS, j * BS : (j + 1) * BS
                ]
        leave(s).start()
        return result

    def half_term(firsts):
        total = jnp.zeros((W2, W2), F32)
        for s, result in firsts:
            total += dot(result, lifted[s])
        return dot(lifted_t[...], total.astype(BF))

    def leave(s):
        return pltpu.make_async_copy(one_ref.at[:, s], one_hbm.at[:, s], store_sem.at[s])

    gives, takes, parts = (give_e, give_l), (take_e, take_l), (part_e, part_l)
    shares, whole = (rs_e, rs_l), (all_e, all_l)

    def pair_copy(w):
        return pltpu.make_async_remote_copy(
            src_ref=gives[w].at[1 - core],
            dst_ref=takes[w],
            send_sem=pair_send.at[w],
            recv_sem=pair_recv.at[w],
            device_id={"row": row, "col": partner},
            device_id_type=MESH,
        )

    def peer(dz):
        return {"row": row, "col": 2 * ((chip + dz) % CHIPS) + core}

    def rs_copy(w, dz):
        return pltpu.make_async_remote_copy(
            src_ref=parts[w].at[(chip + dz) % CHIPS],
            dst_ref=shares[w].at[dz],
            send_sem=rs_send.at[w, dz],
            recv_sem=rs_recv.at[w, dz],
            device_id=peer(dz),
            device_id_type=MESH,
        )

    def ag_copy(w, dz):
        return pltpu.make_async_remote_copy(
            src_ref=whole[w].at[core, chip],
            dst_ref=whole[w].at[core, chip],
            send_sem=ag_send.at[w, dz],
            recv_sem=ag_recv.at[w, dz],
            device_id=peer(dz),
            device_id_type=MESH,
        )

    def ag_arrival(w, dz):
        landing = whole[w].at[core, (chip - dz + CHIPS) % CHIPS]
        return pltpu.make_async_remote_copy(
            src_ref=landing,
            dst_ref=landing,
            send_sem=ag_send.at[w, dz],
            recv_sem=ag_recv.at[w, dz],
            device_id=peer(dz),
            device_id_type=MESH,
        )

    def forward(w, dz):
        piece = whole[w].at[core, (chip - dz + CHIPS) % CHIPS]
        return pltpu.make_async_remote_copy(
            src_ref=piece,
            dst_ref=piece,
            send_sem=fw_send.at[w, dz],
            recv_sem=fw_recv.at[w, dz],
            device_id={"row": row, "col": partner},
            device_id_type=MESH,
        )

    def forward_arrival(w, dz):
        piece = whole[w].at[1 - core, (chip - dz + CHIPS) % CHIPS]
        return pltpu.make_async_remote_copy(
            src_ref=piece,
            dst_ref=piece,
            send_sem=fw_send.at[w, dz],
            recv_sem=fw_recv.at[w, dz],
            device_id={"row": row, "col": partner},
            device_id_type=MESH,
        )

    def scatter(w):
        pair_copy(w).wait_recv()
        total = gives[w][core].astype(F32) + takes[w][...].astype(F32)
        parts[w][...] = total.astype(BF).reshape(CHIPS, HALF[w] // CHIPS, W2)
        for dz in REACH:
            rs_copy(w, dz).start()

    def gather(w):
        total = parts[w][chip].astype(F32)
        for dz in REACH[::-1]:
            rs_copy(w, dz).wait_recv()
            total += shares[w][dz].astype(F32)
        whole[w][core, chip] = total.astype(BF)
        for dz in REACH:
            ag_copy(w, dz).start()
        forward(w, 0).start()

    def hand_over(w):
        for dz in REACH[::-1]:
            ag_arrival(w, dz).wait_recv()
            forward(w, dz).start()

    firsts = [(0, level_one(0))]
    for s in (1, 2):
        arrived(s, 1)
        firsts.append((s, level_one(s)))
    for s in (1, 2):
        arrived(s, 2)
        lift(s)
    early = half_term(firsts).astype(BF)
    for side in range(2):
        give_e[side] = early[side * BS : (side + 1) * BS]
    pair_copy(0).start()
    known(8, 3)
    scatter(0)

    terms = []
    for s in (3, 4):
        arrived(s, 1)
        terms.append(dot(lifted_t[...], level_one(s)).astype(BF))
    for s in (3, 4):
        arrived(s, 2)
        lift(s)
        give_l[s - 3] = dot(terms[s - 3], lifted[s]).astype(BF)
    pair_copy(1).start()
    scatter(1)
    gather(0)
    gather(1)
    hand_over(0)
    hand_over(1)
    leaving = [leave(s) for s in range(5)]
    for w in range(2):
        for dz in range(CHIPS):
            forward_arrival(w, dz).wait_recv()
        last = pltpu.make_async_copy(whole[w], (early_hbm, late_hbm)[w], store_sem.at[5 + w])
        last.start()
        leaving.append(last)
    for s in range(1, 5):

        @pl.when(feeds[s])
        def _():
            for item in range(3):
                halo(s, item).wait_send()

    for w in range(2):
        pair_copy(w).wait_send()
        for dz in REACH:
            rs_copy(w, dz).wait_send()
            ag_copy(w, dz).wait_send()
        for dz in range(CHIPS):
            forward(w, dz).wait_send()
    for copy in leaving:
        copy.wait()


def finish(one_in, early_in, late_in, one_out, two_out, one_v, early_v, late_v, two_v, take, give):
    takes = [
        pltpu.make_async_copy(src, dst, take.at[i])
        for i, (src, dst) in enumerate(((early_in, early_v), (late_in, late_v), (one_in, one_v)))
    ]
    for copy in takes:
        copy.start()
    gives = []
    for g in range(3):
        if g < 2:
            takes[g].wait()
        for a in range(G2):
            if g == 0:
                rows = early_v[a].reshape(BS, W2)
            else:
                rows = late_v[g - 1, a * 4 : a * 4 + 4].reshape(BS, W2)
            for b in range(G2):
                two_v[a, g, b] = rows[:, b * BS : (b + 1) * BS].astype(F32)
        gives.append(pltpu.make_async_copy(two_v.at[:, g], two_out.at[:, g], give.at[g]))
        gives[-1].start()
        if g == 1:
            takes[2].wait()
            gives.append(pltpu.make_async_copy(one_v, one_out, give.at[3]))
            gives[-1].start()
    for copy in gives:
        copy.wait()


def index_rows(*rows):
    out = jnp.zeros((8, BS), jnp.int32)
    for i, row in enumerate(rows):
        if row.shape[1] > 1:
            out += jnp.pad(row, ((i, 7 - i), (0, BS - row.shape[1])))
    at = lax.broadcasted_iota(jnp.int32, (8, BS), 0)
    out = jnp.where(at == 2, rows[2], out)
    return jnp.where(at == 4, rows[4], out)


def per_device(
    fine_blocks,
    fine_rows,
    fine_cols,
    fine_counts,
    prolong_blocks,
    prolong_codes,
    prolong_counts,
    second_blocks,
    second_aggs,
):
    any_spec = pl.BlockSpec(memory_space=pl.ANY)
    dma = pltpu.SemaphoreType.DMA
    meta = index_rows(
        fine_cols[0], fine_rows[0], fine_counts, prolong_codes[0], prolong_counts, second_aggs[0]
    )
    one, early, late = pl.pallas_call(
        kernel,
        name="galerkin",
        out_shape=(
            jax.ShapeDtypeStruct((CB, 5, CB, BS, BS), BF),
            jax.ShapeDtypeStruct((2, CHIPS, HALF[0] // CHIPS, W2), BF),
            jax.ShapeDtypeStruct((2, CHIPS, HALF[1] // CHIPS, W2), BF),
        ),
        in_specs=[any_spec] * 4,
        out_specs=(any_spec,) * 3,
        scratch_shapes=[
            pltpu.VMEM((NA, BS, BS), BF),
            *[pltpu.VMEM((NP + 1, BS, BS), BF)] * 5,
            pltpu.VMEM((5, CB, BS, BS), BF),
            pltpu.VMEM((5, 8, BS), jnp.int32),
            pltpu.SMEM((8, BS), jnp.int32),
            pltpu.VMEM((8, BS), jnp.int32),
            pltpu.SMEM((8, BS), jnp.int32),
            pltpu.VMEM((16, BS), jnp.int32),
            pltpu.SMEM((16, BS), jnp.int32),
            pltpu.VMEM((FB, W2, BS), BF),
            pltpu.VMEM((NA + 1, W2, BS), F32),
            pltpu.VMEM((CB, 5, CB, BS, BS), BF),
            pltpu.VMEM((5, FB // 2, W2, W2), BF),
            pltpu.VMEM((5, W2, W2), BF),
            pltpu.VMEM((W2, W2), BF),
            pltpu.VMEM((2, HALF[0], W2), BF),
            pltpu.VMEM((2, HALF[1], W2), BF),
            pltpu.VMEM((HALF[0], W2), BF),
            pltpu.VMEM((HALF[1], W2), BF),
            pltpu.VMEM((CHIPS, HALF[0] // CHIPS, W2), BF),
            pltpu.VMEM((CHIPS, HALF[1] // CHIPS, W2), BF),
            pltpu.VMEM((CHIPS, HALF[0] // CHIPS, W2), BF),
            pltpu.VMEM((CHIPS, HALF[1] // CHIPS, W2), BF),
            pltpu.VMEM((2, CHIPS, HALF[0] // CHIPS, W2), BF),
            pltpu.VMEM((2, CHIPS, HALF[1] // CHIPS, W2), BF),
            dma((7,)),
            dma((4, 3)),
            dma((4, 3)),
            dma((2,)),
            dma((2,)),
            dma((2, CHIPS)),
            dma((2, CHIPS)),
            dma((2, CHIPS)),
            dma((2, CHIPS)),
            dma((2, CHIPS)),
            dma((2, CHIPS)),
            dma((7,)),
            pltpu.SemaphoreType.REGULAR((4,)),
        ],
        compiler_params=pltpu.CompilerParams(
            collective_id=0, has_side_effects=True, vmem_limit_bytes=VMEM_LIMIT
        ),
    )(
        meta,
        fine_blocks[0, 0],
        prolong_blocks[0, 0],
        second_blocks[0, 0],
    )
    one, two = pl.pallas_call(
        finish,
        name="finish",
        out_shape=(
            jax.ShapeDtypeStruct((CB, 5, CB, BS, BS), BF),
            jax.ShapeDtypeStruct((G2, 3, G2, BS, BS), F32),
        ),
        in_specs=[any_spec] * 3,
        out_specs=(any_spec,) * 2,
        scratch_shapes=[
            pltpu.VMEM((CB, 5, CB, BS, BS), BF),
            pltpu.VMEM((2, CHIPS, HALF[0] // CHIPS, W2), BF),
            pltpu.VMEM((2, CHIPS, HALF[1] // CHIPS, W2), BF),
            pltpu.VMEM((G2, 3, G2, BS, BS), F32),
            dma((3,)),
            dma((4,)),
        ],
    )(one, early, late)
    return (one[None, None], two[None])


def solution(mesh):
    in_specs = (
        P("row", "col", None, None, None),
        P("row", "col", None),
        P("row", "col", None),
        P("row", "col"),
        P("row", "col", None, None, None),
        P("row", "col", None),
        P("row", "col"),
        P("row", "col", None, None, None),
        P("row", "col", None),
    )
    out_specs = (
        P("row", "col", None, None, None, None, None),
        P("row", None, None, None, None, None),
    )
    return jax.shard_map(
        per_device, mesh=mesh, in_specs=in_specs, out_specs=out_specs, check_vma=False
    )
```

```python
import jax
import jax.numpy as jnp
from jax import lax
from jax.experimental import pallas as pl
from jax.experimental.pallas import tpu as pltpu
from jax.sharding import PartitionSpec as P

BS = 128
FB = 8
CB = 2
NA = 64
NP = 12
G2 = 2
NR = 32
NC = 16
CHIPS = NC // 2
W2 = CB * BS
BF = jnp.bfloat16
F32 = jnp.float32
MESH = pl.DeviceIdType.MESH
VMEM_LIMIT = 67043328 - (1088 << 10)
HALF = (BS, 2 * BS)
REACH = (4, 3, 5, 2, 6, 1, 7)
GROUPS = ((1, 7, 2, 6), (3, 5), (4,))


def dot(a, b):
    return jnp.dot(a, b, preferred_element_type=F32)


def kernel(
    cols_hbm,
    rows_hbm,
    fcount_s,
    codes_hbm,
    pcount_s,
    aggs_hbm,
    a_hbm,
    p_hbm,
    l_hbm,
    one_ref,
    all_e,
    all_l,
    a_buf,
    p_0,
    p_1,
    p_2,
    p_3,
    p_4,
    l_buf,
    meta_v,
    cols_v,
    codes_v,
    aggs_v,
    rows_s,
    table_v,
    table_s,
    near_v,
    near_s,
    pt,
    run,
    wide,
    lifted,
    lifted_t,
    give_e,
    give_l,
    take_e,
    take_l,
    part_e,
    part_l,
    rs_e,
    rs_l,
    load_sem,
    halo_send,
    halo_recv,
    pair_send,
    pair_recv,
    rs_send,
    rs_recv,
    ag_send,
    ag_recv,
    fw_send,
    fw_recv,
    reach_sem,
):
    p_bufs = (p_0, p_1, p_2, p_3, p_4)
    row = lax.axis_index("row")
    col = lax.axis_index("col")
    chip = col // 2
    core = col % 2
    partner = 2 * chip + 1 - core

    def at(dr, dc):
        return {"row": (row + dr + NR) % NR, "col": (col + dc + NC) % NC}

    sources = ((0, -1), (0, 1), (-1, 0), (1, 0))

    has = (None, col > 0, col < NC - 1, row > 0, row < NR - 1)
    feeds = (None, has[2], has[1], has[4], has[3])

    barrier = pltpu.get_barrier_semaphore()
    for (dr, dc), near in zip(sources, has[1:]):

        @pl.when(near)
        def _():
            pl.semaphore_signal(barrier, inc=1, device_id=at(dr, dc), device_id_type=MESH)


    loads = [
        pltpu.make_async_copy(codes_hbm, codes_v, load_sem.at[0]),
        pltpu.make_async_copy(aggs_hbm, aggs_v, load_sem.at[1]),
        pltpu.make_async_copy(cols_hbm, cols_v, load_sem.at[2]),
        pltpu.make_async_copy(rows_hbm, rows_s, load_sem.at[3]),
        pltpu.make_async_copy(p_hbm, p_0.at[pl.ds(0, NP)], load_sem.at[4]),
        pltpu.make_async_copy(l_hbm, l_buf.at[0], load_sem.at[5]),
        pltpu.make_async_copy(a_hbm, a_buf, load_sem.at[6]),
    ]
    for load in loads:
        load.start()
    for s in range(5):
        p_bufs[s][NP] = jnp.zeros((BS, BS), BF)
    run[NA] = jnp.zeros((W2, BS), F32)

    for s in range(1, 5):

        @pl.when(jnp.logical_not(has[s]))
        def _():
            meta_v[s] = jnp.zeros((8, BS), jnp.int32)
            l_buf[s] = jnp.zeros((CB, BS, BS), BF)

    meta_v[0] = jnp.zeros((8, BS), jnp.int32)
    meta_v[0, 1:2] = jnp.full((1, BS), pcount_s[0, 0], jnp.int32)
    loads[0].wait()
    meta_v[0, 0:1, 0:NP] = codes_v[0]
    loads[1].wait()
    meta_v[0, 2:3, 0:CB] = aggs_v[0]

    pl.semaphore_wait(barrier, sum(near.astype(jnp.int32) for near in has[1:]))

    def halo(s, item):
        src, dst = (
            (meta_v.at[0], meta_v.at[s]),
            (p_hbm, p_bufs[s].at[pl.ds(0, NP)]),
            (l_hbm, l_buf.at[s]),
        )[item]
        dr, dc = sources[s - 1]
        return pltpu.make_async_remote_copy(
            src_ref=src,
            dst_ref=dst,
            send_sem=halo_send.at[s - 1, min(item, 1)],
            recv_sem=halo_recv.at[s - 1, item],
            device_id=at(-dr, -dc),
            device_id_type=MESH,
        )

    order = (3, 4, 1, 2)
    for item in range(3):
        for s in order:

            @pl.when(feeds[s])
            def _():
                halo(s, item).start()

    def arrived(s, item):
        @pl.when(has[s])
        def _():
            halo(s, item).wait_recv()


    def spread(step, slot):
        for sign in (-1, 1):

            @pl.when((col + sign * step >= 0) & (col + sign * step < NC))
            def _():
                pl.semaphore_signal(
                    reach_sem.at[slot], inc=1, device_id=at(0, sign * step), device_id_type=MESH
                )

    def known(step, slot):
        ends = (col >= step).astype(jnp.int32) + (col < NC - step).astype(jnp.int32)
        pl.semaphore_wait(reach_sem.at[slot], ends)

    spread(1, 0)

    sub = lax.broadcasted_iota(jnp.int32, (BS, BS), 0)
    lane = lax.broadcasted_iota(jnp.int32, (BS, BS), 1)

    def down(vector, length):
        diag = sub[:length] == lane[:length]
        return jnp.max(jnp.where(diag, vector, -1), axis=1, keepdims=True)

    def pick(match, length, missing):
        best = jnp.max(jnp.where(match, sub[:length], -1), axis=0, keepdims=True)
        return jnp.where(best < 0, missing, best)

    def place(s):
        codes_down = down(meta_v[s, 0:1], 16)
        return pick((codes_down == lane[:16]) & (sub[:16] < meta_v[s, 1:2]), 16, NP)

    loads[2].wait()
    cols = jnp.concatenate([cols_v[0], cols_v[0]], axis=1)
    cols_down = down(cols, NA)
    live = sub[:NA] < fcount_s[0, 0]
    table_v[0:1] = pick((cols_down == cols) & (sub[:NA] < lane[:NA]) & live, NA, NA)
    table_v[1:2] = pick((cols_down == lane[:NA]) & live, NA, NA)
    table_v[2:3] = place(0)
    send_table = pltpu.make_async_copy(table_v, table_s, load_sem.at[7])
    send_table.start()
    loads[4].wait()
    for slot in range(NP + 1):
        pt[slot] = p_0[slot].T
    loads[3].wait()
    send_table.wait()
    known(1, 0)
    spread(2, 1)
    loads[6].wait()

    def slots(step, carry):
        for inner in range(4):
            k = step * 4 + inner
            i = rows_s[0, 0, k]
            own = jnp.concatenate([pt[table_s[2, i * CB + j]] for j in range(CB)], axis=0)
            run[k] = dot(own, a_buf[k]) + run[table_s[0, k]]
        return carry

    lax.fori_loop(0, 12, slots, 0)
    known(2, 1)
    spread(4, 2)
    for s in range(1, 5):
        arrived(s, 0)
    near_v[0:1] = table_v[2:3]
    near_v[8:9] = meta_v[0, 2:3]
    for s in range(1, 5):
        near_v[s : s + 1] = place(s)
        near_v[8 + s : 9 + s] = meta_v[s, 2:3]
    send_near = pltpu.make_async_copy(near_v, near_s, load_sem.at[8])
    send_near.start()
    lax.fori_loop(12, NA // 4, slots, 0)
    known(4, 2)
    spread(8, 3)

    def widen_rows(s, carry):
        for m in range(FB):
            slot = table_s[1, s * FB + m]
            wide[s, m // 2, :, pl.ds((m % 2) * BS, BS)] = run[slot].astype(BF)
        return carry

    lax.fori_loop(0, 5, widen_rows, 0)
    loads[5].wait()
    send_near.wait()

    def lift(s):
        for j in range(CB):
            block = l_buf[s, j]
            for a in range(G2):
                kept = jnp.where(near_s[8 + s, j] == a, block, jnp.zeros_like(block))
                lifted[s, pl.ds(j * BS, BS), pl.ds(a * BS, BS)] = kept

    lift(0)
    lifted_t[...] = lifted[0].T

    def level_one(s):
        total = jnp.zeros((W2, W2), F32)
        for pair in range(FB // 2):
            right = jnp.concatenate(
                [
                    jnp.concatenate(
                        [p_bufs[s][near_s[s, (2 * pair + low) * CB + j]] for j in range(CB)], axis=1
                    )
                    for low in range(2)
                ],
                axis=0,
            )
            total += dot(wide[s, pair], right)
        result = total.astype(BF)
        for coarse in range(CB):
            for j in range(CB):
                one_ref[coarse, s, j] = result[
                    coarse * BS : (coarse + 1) * BS, j * BS : (j + 1) * BS
                ]
        return result

    def half_term(firsts):
        total = jnp.zeros((W2, W2), F32)
        for s, result in firsts:
            total += dot(result, lifted[s])
        return dot(lifted_t[...], total.astype(BF))

    gives, takes, parts = (give_e, give_l), (take_e, take_l), (part_e, part_l)
    shares, whole = (rs_e, rs_l), (all_e, all_l)

    def pair_copy(w):
        return pltpu.make_async_remote_copy(
            src_ref=gives[w].at[1 - core],
            dst_ref=takes[w],
            send_sem=pair_send.at[w],
            recv_sem=pair_recv.at[w],
            device_id={"row": row, "col": partner},
            device_id_type=MESH,
        )

    def peer(dz):
        return {"row": row, "col": 2 * ((chip + dz) % CHIPS) + core}

    def rs_copy(w, dz):
        return pltpu.make_async_remote_copy(
            src_ref=parts[w].at[(chip + dz) % CHIPS],
            dst_ref=shares[w].at[dz - 1],
            send_sem=rs_send.at[w],
            recv_sem=rs_recv.at[w],
            device_id=peer(dz),
            device_id_type=MESH,
        )

    def together(ref, count, send_sem, recv_sem):
        part = ref.at[pl.ds(0, count)]
        return pltpu.make_async_remote_copy(
            src_ref=part,
            dst_ref=part,
            send_sem=send_sem,
            recv_sem=recv_sem,
            device_id=peer(1),
            device_id_type=MESH,
        )

    def ag_copy(w, dz, group):
        return pltpu.make_async_remote_copy(
            src_ref=whole[w].at[core, chip],
            dst_ref=whole[w].at[core, chip],
            send_sem=ag_send.at[w],
            recv_sem=ag_recv.at[w, group],
            device_id=peer(dz),
            device_id_type=MESH,
        )

    def forward(w, dz):
        piece = whole[w].at[core, (chip - dz + CHIPS) % CHIPS]
        return pltpu.make_async_remote_copy(
            src_ref=piece,
            dst_ref=piece,
            send_sem=fw_send.at[w],
            recv_sem=fw_recv.at[w],
            device_id={"row": row, "col": partner},
            device_id_type=MESH,
        )

    def scatter(w):
        pair_copy(w).wait_recv()
        total = gives[w][core].astype(F32) + takes[w][...].astype(F32)
        parts[w][...] = total.astype(BF).reshape(CHIPS, HALF[w] // CHIPS, W2)
        for dz in REACH:
            rs_copy(w, dz).start()

    def gather(w):
        together(shares[w], CHIPS - 1, rs_send.at[w], rs_recv.at[w]).wait_recv()
        total = parts[w][chip].astype(F32)
        for dz in range(1, CHIPS):
            total += shares[w][dz - 1].astype(F32)
        whole[w][core, chip] = total.astype(BF)
        for group in (2, 1, 0):
            for dz in GROUPS[group]:
                ag_copy(w, dz, group).start()
        forward(w, 0).start()

    def hand_over(w, group):
        count = len(GROUPS[group])
        together(whole[w].at[core], count, ag_send.at[w], ag_recv.at[w, group]).wait_recv()
        for dz in GROUPS[group]:
            forward(w, dz).start()

    firsts = [(0, level_one(0))]
    for s in (1, 2):
        arrived(s, 1)
        firsts.append((s, level_one(s)))
    for s in (1, 2):
        arrived(s, 2)
        lift(s)
    early = half_term(firsts).astype(BF)
    for side in range(2):
        give_e[side] = early[side * BS : (side + 1) * BS]
    pair_copy(0).start()
    known(8, 3)
    scatter(0)

    terms = []
    for s in (3, 4):
        arrived(s, 1)
        terms.append(dot(lifted_t[...], level_one(s)).astype(BF))
    for s in (3, 4):
        arrived(s, 2)
        lift(s)
        give_l[s - 3] = dot(terms[s - 3], lifted[s]).astype(BF)
    pair_copy(1).start()
    scatter(1)
    gather(0)
    gather(1)
    for group in range(3):
        hand_over(0, group)
    for group in range(3):
        hand_over(1, group)
    for s in range(1, 5):

        @pl.when(feeds[s])
        def _():
            halo(s, 0).wait_send()
            together(a_buf, NP + CB, halo_send.at[s - 1, 1], halo_recv.at[s - 1, 1]).wait_send()

    for w in range(2):
        pair_copy(w).wait_send()
        together(parts[w], CHIPS - 1, rs_send.at[w], rs_recv.at[w]).wait_send()
        together(whole[w].at[core], CHIPS - 1, ag_send.at[w], ag_recv.at[w, 0]).wait_send()
        together(whole[w].at[core], CHIPS, fw_send.at[w], fw_recv.at[w]).wait_send()
    for w in range(2):
        together(whole[w].at[1 - core], CHIPS, fw_send.at[w], fw_recv.at[w]).wait_recv()


def finish(one_v, early_v, late_v, one_out, two_out, two_v, give):
    gives = [pltpu.make_async_copy(one_v, one_out, give.at[3])]
    gives[0].start()
    for g in range(3):
        for a in range(G2):
            if g == 0:
                rows = early_v[a].reshape(BS, W2)
            else:
                rows = late_v[g - 1, a * 4 : a * 4 + 4].reshape(BS, W2)
            for b in range(G2):
                two_v[a, g, b] = rows[:, b * BS : (b + 1) * BS].astype(F32)
        gives.append(pltpu.make_async_copy(two_v.at[:, g], two_out.at[:, g], give.at[g]))
        gives[-1].start()
    for copy in gives:
        copy.wait()


def per_device(
    fine_blocks,
    fine_rows,
    fine_cols,
    fine_counts,
    prolong_blocks,
    prolong_codes,
    prolong_counts,
    second_blocks,
    second_aggs,
):
    any_spec = pl.BlockSpec(memory_space=pl.ANY)
    vmem = pl.BlockSpec(memory_space=pltpu.VMEM)
    smem = pl.BlockSpec(memory_space=pltpu.SMEM)
    dma = pltpu.SemaphoreType.DMA
    one, early, late = pl.pallas_call(
        kernel,
        name="galerkin",
        out_shape=(
            pltpu.VMEM((CB, 5, CB, BS, BS), BF),
            pltpu.VMEM((2, CHIPS, HALF[0] // CHIPS, W2), BF),
            pltpu.VMEM((2, CHIPS, HALF[1] // CHIPS, W2), BF),
        ),
        in_specs=[any_spec] * 2 + [smem, any_spec] * 2 + [any_spec] * 3,
        out_specs=(vmem,) * 3,
        scratch_shapes=[
            pltpu.VMEM((NA, BS, BS), BF),
            *[pltpu.VMEM((NP + 1, BS, BS), BF)] * 5,
            pltpu.VMEM((5, CB, BS, BS), BF),
            pltpu.VMEM((5, 8, BS), jnp.int32),
            pltpu.VMEM((1, 1, NA), jnp.int32),
            pltpu.VMEM((1, 1, NP), jnp.int32),
            pltpu.VMEM((1, 1, CB), jnp.int32),
            pltpu.SMEM((1, 1, NA), jnp.int32),
            pltpu.VMEM((8, BS), jnp.int32),
            pltpu.SMEM((8, BS), jnp.int32),
            pltpu.VMEM((16, BS), jnp.int32),
            pltpu.SMEM((16, BS), jnp.int32),
            pltpu.VMEM((NP + 1, BS, BS), BF),
            pltpu.VMEM((NA + 1, W2, BS), F32),
            pltpu.VMEM((5, FB // 2, W2, W2), BF),
            pltpu.VMEM((5, W2, W2), BF),
            pltpu.VMEM((W2, W2), BF),
            pltpu.VMEM((2, HALF[0], W2), BF),
            pltpu.VMEM((2, HALF[1], W2), BF),
            pltpu.VMEM((HALF[0], W2), BF),
            pltpu.VMEM((HALF[1], W2), BF),
            pltpu.VMEM((CHIPS, HALF[0] // CHIPS, W2), BF),
            pltpu.VMEM((CHIPS, HALF[1] // CHIPS, W2), BF),
            pltpu.VMEM((CHIPS - 1, HALF[0] // CHIPS, W2), BF),
            pltpu.VMEM((CHIPS - 1, HALF[1] // CHIPS, W2), BF),
            dma((9,)),
            dma((4, 2)),
            dma((4, 3)),
            dma((2,)),
            dma((2,)),
            dma((2,)),
            dma((2,)),
            dma((2,)),
            dma((2, 3)),
            dma((2,)),
            dma((2,)),
            pltpu.SemaphoreType.REGULAR((4,)),
        ],
        compiler_params=pltpu.CompilerParams(
            collective_id=0, has_side_effects=True, vmem_limit_bytes=VMEM_LIMIT
        ),
    )(
        fine_cols,
        fine_rows,
        fine_counts,
        prolong_codes,
        prolong_counts,
        second_aggs,
        fine_blocks[0, 0],
        prolong_blocks[0, 0],
        second_blocks[0, 0],
    )
    one, two = pl.pallas_call(
        finish,
        name="finish",
        out_shape=(
            jax.ShapeDtypeStruct((CB, 5, CB, BS, BS), BF),
            jax.ShapeDtypeStruct((G2, 3, G2, BS, BS), F32),
        ),
        in_specs=[vmem] * 3,
        out_specs=(any_spec,) * 2,
        scratch_shapes=[pltpu.VMEM((G2, 3, G2, BS, BS), F32), dma((4,))],
    )(*(pltpu.with_memory_space_constraint(x, pltpu.VMEM) for x in (one, early, late)))
    return (one[None, None], two[None])


def solution(mesh):
    in_specs = (
        P("row", "col", None, None, None),
        P("row", "col", None),
        P("row", "col", None),
        P("row", "col"),
        P("row", "col", None, None, None),
        P("row", "col", None),
        P("row", "col"),
        P("row", "col", None, None, None),
        P("row", "col", None),
    )
    out_specs = (
        P("row", "col", None, None, None, None, None),
        P("row", None, None, None, None, None),
    )
    return jax.shard_map(
        per_device, mesh=mesh, in_specs=in_specs, out_specs=out_specs, check_vma=False
    )
```

```python
import jax
import jax.numpy as jnp
from jax import lax
from jax.experimental import pallas as pl
from jax.experimental.pallas import tpu as pltpu
from jax.sharding import PartitionSpec as P

BS = 128
FB = 8
CB = 2
NA = 64
NP = 12
G2 = 2
NR = 32
NC = 16
CHIPS = NC // 2
W2 = CB * BS
BF = jnp.bfloat16
F32 = jnp.float32
MESH = pl.DeviceIdType.MESH
VMEM_LIMIT = 67043328 - (1088 << 10)
HALF = (BS, 2 * BS)
REACH = (4, 3, 5, 2, 6, 1, 7)
GROUPS = ((1, 7, 2, 6), (3, 5), (4,))


def dot(a, b):
    return jnp.dot(a, b, preferred_element_type=F32)


def kernel(
    cols_hbm,
    rows_hbm,
    fcount_s,
    codes_hbm,
    pcount_s,
    aggs_hbm,
    a_hbm,
    p_hbm,
    l_hbm,
    one_ref,
    all_e,
    all_l,
    a_buf,
    p_0,
    p_1,
    p_2,
    p_row,
    l_buf,
    meta_v,
    cols_v,
    codes_v,
    aggs_v,
    rows_s,
    table_v,
    table_s,
    near_v,
    near_s,
    pt,
    run,
    wide,
    folded,
    lifted,
    lifted_t,
    give_e,
    give_l,
    take_e,
    take_l,
    part_e,
    part_l,
    rs_e,
    rs_l,
    load_sem,
    halo_send,
    halo_recv,
    pair_send,
    pair_recv,
    rs_send,
    rs_recv,
    ag_send,
    ag_recv,
    fw_send,
    fw_recv,
    reach_sem,
):
    p_bufs = (p_0, p_1, p_2, p_row.at[0], p_row.at[1])
    row = lax.axis_index("row")
    col = lax.axis_index("col")
    chip = col // 2
    core = col % 2
    partner = 2 * chip + 1 - core

    def at(dr, dc):
        return {"row": (row + dr + NR) % NR, "col": (col + dc + NC) % NC}

    sources = ((0, -1), (0, 1), (-1, 0), (1, 0))

    has = (None, col > 0, col < NC - 1, row > 0, row < NR - 1)
    feeds = (None, has[2], has[1], has[4], has[3])

    barrier = pltpu.get_barrier_semaphore()
    for (dr, dc), near in zip(sources, has[1:]):

        @pl.when(near)
        def _():
            pl.semaphore_signal(barrier, inc=1, device_id=at(dr, dc), device_id_type=MESH)


    loads = [
        pltpu.make_async_copy(codes_hbm, codes_v, load_sem.at[0]),
        pltpu.make_async_copy(aggs_hbm, aggs_v, load_sem.at[1]),
        pltpu.make_async_copy(cols_hbm, cols_v, load_sem.at[2]),
        pltpu.make_async_copy(rows_hbm, rows_s, load_sem.at[3]),
        pltpu.make_async_copy(p_hbm, p_0.at[pl.ds(0, NP)], load_sem.at[4]),
        pltpu.make_async_copy(l_hbm, l_buf.at[0], load_sem.at[5]),
        pltpu.make_async_copy(a_hbm, a_buf, load_sem.at[6]),
    ]
    for load in loads:
        load.start()
    for s in range(5):
        p_bufs[s][NP] = jnp.zeros((BS, BS), BF)
    run[NA] = jnp.zeros((W2, BS), F32)

    for s in range(1, 5):

        @pl.when(jnp.logical_not(has[s]))
        def _():
            meta_v[s] = jnp.zeros((8, BS), jnp.int32)
            l_buf[s] = jnp.zeros((CB, BS, BS), BF)

    meta_v[0] = jnp.zeros((8, BS), jnp.int32)
    meta_v[0, 1:2] = jnp.full((1, BS), pcount_s[0, 0], jnp.int32)
    loads[0].wait()
    meta_v[0, 0:1, 0:NP] = codes_v[0]
    loads[1].wait()
    meta_v[0, 2:3, 0:CB] = aggs_v[0]

    pl.semaphore_wait(barrier, sum(near.astype(jnp.int32) for near in has[1:]))

    def halo(s, item):
        src, dst = (
            (meta_v.at[0], meta_v.at[s]),
            (p_0.at[pl.ds(0, NP)], p_bufs[s].at[pl.ds(0, NP)]),
            (l_buf.at[0], l_buf.at[s]),
        )[item]
        dr, dc = sources[s - 1]
        return pltpu.make_async_remote_copy(
            src_ref=src,
            dst_ref=dst,
            send_sem=halo_send.at[s - 1, min(item, 1)],
            recv_sem=halo_recv.at[s - 1, item],
            device_id=at(-dr, -dc),
            device_id_type=MESH,
        )

    loads[4].wait()
    loads[5].wait()
    order = (3, 4, 1, 2)
    for item in range(3):
        for s in order:

            @pl.when(feeds[s])
            def _():
                halo(s, item).start()

    def arrived(s, item):
        @pl.when(has[s])
        def _():
            halo(s, item).wait_recv()


    def spread(step, slot):
        for sign in (-1, 1):

            @pl.when((col + sign * step >= 0) & (col + sign * step < NC))
            def _():
                pl.semaphore_signal(
                    reach_sem.at[slot], inc=1, device_id=at(0, sign * step), device_id_type=MESH
                )

    def known(step, slot):
        ends = (col >= step).astype(jnp.int32) + (col < NC - step).astype(jnp.int32)
        pl.semaphore_wait(reach_sem.at[slot], ends)

    spread(1, 0)

    sub = lax.broadcasted_iota(jnp.int32, (BS, BS), 0)
    lane = lax.broadcasted_iota(jnp.int32, (BS, BS), 1)

    def down(vector, length):
        diag = sub[:length] == lane[:length]
        return jnp.max(jnp.where(diag, vector, -1), axis=1, keepdims=True)

    def pick(match, length, missing):
        best = jnp.max(jnp.where(match, sub[:length], -1), axis=0, keepdims=True)
        return jnp.where(best < 0, missing, best)

    def place(s):
        codes_down = down(meta_v[s, 0:1], 16)
        return pick((codes_down == lane[:16]) & (sub[:16] < meta_v[s, 1:2]), 16, NP)

    loads[2].wait()
    cols = jnp.concatenate([cols_v[0], cols_v[0]], axis=1)
    cols_down = down(cols, NA)
    live = sub[:NA] < fcount_s[0, 0]
    table_v[0:1] = pick((cols_down == cols) & (sub[:NA] < lane[:NA]) & live, NA, NA)
    table_v[1:2] = pick((cols_down == lane[:NA]) & live, NA, NA)
    table_v[2:3] = place(0)
    send_table = pltpu.make_async_copy(table_v, table_s, load_sem.at[7])
    send_table.start()
    for slot in range(NP + 1):
        pt[slot] = p_0[slot].T
    loads[3].wait()
    send_table.wait()
    known(1, 0)
    spread(2, 1)
    loads[6].wait()

    def slots(step, carry):
        for inner in range(4):
            k = step * 4 + inner
            i = rows_s[0, 0, k]
            own = jnp.concatenate([pt[table_s[2, i * CB + j]] for j in range(CB)], axis=0)
            run[k] = dot(own, a_buf[k]) + run[table_s[0, k]]
        return carry

    lax.fori_loop(0, 4, slots, 0)
    known(2, 1)
    spread(4, 2)
    lax.fori_loop(4, 12, slots, 0)
    known(4, 2)
    spread(8, 3)
    for s in range(1, 5):
        arrived(s, 0)
    near_v[0:1] = table_v[2:3]
    near_v[8:9] = meta_v[0, 2:3]
    for s in range(1, 5):
        near_v[s : s + 1] = place(s)
        near_v[8 + s : 9 + s] = meta_v[s, 2:3]
    send_near = pltpu.make_async_copy(near_v, near_s, load_sem.at[8])
    send_near.start()
    lax.fori_loop(12, NA // 4, slots, 0)

    def widen_rows(s, carry):
        for m in range(FB):
            slot = table_s[1, s * FB + m]
            wide[s, m // 2, :, pl.ds((m % 2) * BS, BS)] = run[slot].astype(BF)
        return carry

    lax.fori_loop(0, 5, widen_rows, 0)
    send_near.wait()

    def lift(s):
        for j in range(CB):
            block = l_buf[s, j]
            for a in range(G2):
                kept = jnp.where(near_s[8 + s, j] == a, block, jnp.zeros_like(block))
                lifted[s, pl.ds(j * BS, BS), pl.ds(a * BS, BS)] = kept

    lift(0)
    lifted_t[...] = lifted[0].T

    def dense(block, s, pair):
        return jnp.concatenate(
            [
                jnp.concatenate(
                    [block(near_s[s, (2 * pair + low) * CB + j]) for j in range(CB)], axis=1
                )
                for low in range(2)
            ],
            axis=0,
        )

    def level_one(s):
        total = jnp.zeros((W2, W2), F32)
        for pair in range(FB // 2):
            total += dot(wide[s, pair], dense(lambda slot: p_bufs[s][slot], s, pair))
        result = total.astype(BF)
        for coarse in range(CB):
            for j in range(CB):
                one_ref[coarse, s, j] = result[
                    coarse * BS : (coarse + 1) * BS, j * BS : (j + 1) * BS
                ]
        return result

    def late_half(d):
        total = jnp.zeros((W2, W2), F32)
        for pair in range(FB // 2):
            total += dot(folded[d, pair], dense(lambda slot: p_row[d, slot], 3 + d, pair))
        return total.astype(BF)

    def half_term(firsts):
        total = jnp.zeros((W2, W2), F32)
        for s, result in firsts:
            total += dot(result, lifted[s])
        return dot(lifted_t[...], total.astype(BF))

    takes, parts = (take_e, take_l), (part_e, part_l)
    shares, whole = (rs_e, rs_l), (all_e, all_l)

    def pair_copy(w):
        return pltpu.make_async_remote_copy(
            src_ref=give_l if w else give_e.at[1 - core],
            dst_ref=takes[w],
            send_sem=pair_send.at[w],
            recv_sem=pair_recv.at[w],
            device_id={"row": row, "col": partner},
            device_id_type=MESH,
        )

    def peer(dz):
        return {"row": row, "col": 2 * ((chip + dz) % CHIPS) + core}

    def rs_copy(w, dz):
        return pltpu.make_async_remote_copy(
            src_ref=parts[w].at[(chip + dz) % CHIPS],
            dst_ref=shares[w].at[dz - 1],
            send_sem=rs_send.at[w],
            recv_sem=rs_recv.at[w],
            device_id=peer(dz),
            device_id_type=MESH,
        )

    def together(ref, count, send_sem, recv_sem):
        part = ref.at[pl.ds(0, count)]
        return pltpu.make_async_remote_copy(
            src_ref=part,
            dst_ref=part,
            send_sem=send_sem,
            recv_sem=recv_sem,
            device_id=peer(1),
            device_id_type=MESH,
        )

    def ag_copy(w, dz, group):
        return pltpu.make_async_remote_copy(
            src_ref=whole[w].at[core, chip],
            dst_ref=whole[w].at[core, chip],
            send_sem=ag_send.at[w],
            recv_sem=ag_recv.at[w, group],
            device_id=peer(dz),
            device_id_type=MESH,
        )

    def forward(w, dz):
        piece = whole[w].at[core, (chip - dz + CHIPS) % CHIPS]
        return pltpu.make_async_remote_copy(
            src_ref=piece,
            dst_ref=piece,
            send_sem=fw_send.at[w],
            recv_sem=fw_recv.at[w],
            device_id={"row": row, "col": partner},
            device_id_type=MESH,
        )

    def scatter(w, own):
        pair_copy(w).wait_recv()
        total = own + takes[w][...].astype(F32)
        parts[w][...] = total.astype(BF).reshape(CHIPS, HALF[w] // CHIPS, W2)
        for dz in REACH:
            rs_copy(w, dz).start()

    def gather(w):
        together(shares[w], CHIPS - 1, rs_send.at[w], rs_recv.at[w]).wait_recv()
        total = parts[w][chip].astype(F32)
        for dz in range(1, CHIPS):
            total += shares[w][dz - 1].astype(F32)
        whole[w][core, chip] = total.astype(BF)
        for group in (2, 1, 0):
            for dz in GROUPS[group]:
                ag_copy(w, dz, group).start()
        forward(w, 0).start()

    def hand_over(w, group):
        count = len(GROUPS[group])
        together(whole[w].at[core], count, ag_send.at[w], ag_recv.at[w, group]).wait_recv()
        for dz in GROUPS[group]:
            forward(w, dz).start()

    firsts = [(0, level_one(0))]
    for s in (1, 2):
        arrived(s, 1)
        firsts.append((s, level_one(s)))
    for s in (1, 2):
        arrived(s, 2)
        lift(s)
    early = half_term(firsts).astype(BF)
    for side in range(2):
        give_e[side] = early[side * BS : (side + 1) * BS]
    pair_copy(0).start()
    known(8, 3)
    scatter(0, give_e[core].astype(F32))

    for d in range(2):
        for pair in range(FB // 2):
            folded[d, pair] = dot(lifted_t[...], wide[3 + d, pair]).astype(BF)
    for s in (3, 4):
        arrived(s, 1)
    away, kept = late_half(1 - core), late_half(core)
    for s in (3, 4):
        arrived(s, 2)
        lift(s)
    give_l[...] = dot(away, lifted[4 - core]).astype(BF)
    pair_copy(1).start()
    own = dot(kept, lifted[3 + core])
    scatter(1, own)
    gather(0)
    for s in (3, 4):
        level_one(s)
    gather(1)
    for group in range(3):
        hand_over(0, group)
    for group in range(3):
        hand_over(1, group)
    for s in range(1, 5):

        @pl.when(feeds[s])
        def _():
            halo(s, 0).wait_send()
            together(a_buf, NP + CB, halo_send.at[s - 1, 1], halo_recv.at[s - 1, 1]).wait_send()

    for w in range(2):
        pair_copy(w).wait_send()
        together(parts[w], CHIPS - 1, rs_send.at[w], rs_recv.at[w]).wait_send()
        together(whole[w].at[core], CHIPS - 1, ag_send.at[w], ag_recv.at[w, 0]).wait_send()
        together(whole[w].at[core], CHIPS, fw_send.at[w], fw_recv.at[w]).wait_send()
    for w in range(2):
        together(whole[w].at[1 - core], CHIPS, fw_send.at[w], fw_recv.at[w]).wait_recv()


def finish(one_v, early_v, late_v, one_out, two_out, two_v, give):
    gives = [pltpu.make_async_copy(one_v, one_out, give.at[3])]
    gives[0].start()
    for g in range(3):
        for a in range(G2):
            if g == 0:
                rows = early_v[a].reshape(BS, W2)
            else:
                rows = late_v[g - 1, a * 4 : a * 4 + 4].reshape(BS, W2)
            for b in range(G2):
                two_v[a, g, b] = rows[:, b * BS : (b + 1) * BS].astype(F32)
        gives.append(pltpu.make_async_copy(two_v.at[:, g], two_out.at[:, g], give.at[g]))
        gives[-1].start()
    for copy in gives:
        copy.wait()


def per_device(
    fine_blocks,
    fine_rows,
    fine_cols,
    fine_counts,
    prolong_blocks,
    prolong_codes,
    prolong_counts,
    second_blocks,
    second_aggs,
):
    any_spec = pl.BlockSpec(memory_space=pl.ANY)
    vmem = pl.BlockSpec(memory_space=pltpu.VMEM)
    smem = pl.BlockSpec(memory_space=pltpu.SMEM)
    dma = pltpu.SemaphoreType.DMA
    one, early, late = pl.pallas_call(
        kernel,
        name="galerkin",
        out_shape=(
            pltpu.VMEM((CB, 5, CB, BS, BS), BF),
            pltpu.VMEM((2, CHIPS, HALF[0] // CHIPS, W2), BF),
            pltpu.VMEM((2, CHIPS, HALF[1] // CHIPS, W2), BF),
        ),
        in_specs=[any_spec] * 2 + [smem, any_spec] * 2 + [any_spec] * 3,
        out_specs=(vmem,) * 3,
        scratch_shapes=[
            pltpu.VMEM((NA, BS, BS), BF),
            *[pltpu.VMEM((NP + 1, BS, BS), BF)] * 3,
            pltpu.VMEM((2, NP + 1, BS, BS), BF),
            pltpu.VMEM((5, CB, BS, BS), BF),
            pltpu.VMEM((5, 8, BS), jnp.int32),
            pltpu.VMEM((1, 1, NA), jnp.int32),
            pltpu.VMEM((1, 1, NP), jnp.int32),
            pltpu.VMEM((1, 1, CB), jnp.int32),
            pltpu.SMEM((1, 1, NA), jnp.int32),
            pltpu.VMEM((8, BS), jnp.int32),
            pltpu.SMEM((8, BS), jnp.int32),
            pltpu.VMEM((16, BS), jnp.int32),
            pltpu.SMEM((16, BS), jnp.int32),
            pltpu.VMEM((NP + 1, BS, BS), BF),
            pltpu.VMEM((NA + 1, W2, BS), F32),
            pltpu.VMEM((5, FB // 2, W2, W2), BF),
            pltpu.VMEM((2, FB // 2, W2, W2), BF),
            pltpu.VMEM((5, W2, W2), BF),
            pltpu.VMEM((W2, W2), BF),
            pltpu.VMEM((2, HALF[0], W2), BF),
            pltpu.VMEM((HALF[1], W2), BF),
            pltpu.VMEM((HALF[0], W2), BF),
            pltpu.VMEM((HALF[1], W2), BF),
            pltpu.VMEM((CHIPS, HALF[0] // CHIPS, W2), BF),
            pltpu.VMEM((CHIPS, HALF[1] // CHIPS, W2), BF),
            pltpu.VMEM((CHIPS - 1, HALF[0] // CHIPS, W2), BF),
            pltpu.VMEM((CHIPS - 1, HALF[1] // CHIPS, W2), BF),
            dma((9,)),
            dma((4, 2)),
            dma((4, 3)),
            dma((2,)),
            dma((2,)),
            dma((2,)),
            dma((2,)),
            dma((2,)),
            dma((2, 3)),
            dma((2,)),
            dma((2,)),
            pltpu.SemaphoreType.REGULAR((4,)),
        ],
        compiler_params=pltpu.CompilerParams(
            collective_id=0, has_side_effects=True, vmem_limit_bytes=VMEM_LIMIT
        ),
    )(
        fine_cols,
        fine_rows,
        fine_counts,
        prolong_codes,
        prolong_counts,
        second_aggs,
        fine_blocks[0, 0],
        prolong_blocks[0, 0],
        second_blocks[0, 0],
    )
    one, two = pl.pallas_call(
        finish,
        name="finish",
        out_shape=(
            jax.ShapeDtypeStruct((CB, 5, CB, BS, BS), BF),
            jax.ShapeDtypeStruct((G2, 3, G2, BS, BS), F32),
        ),
        in_specs=[vmem] * 3,
        out_specs=(any_spec,) * 2,
        scratch_shapes=[pltpu.VMEM((G2, 3, G2, BS, BS), F32), dma((4,))],
    )(*(pltpu.with_memory_space_constraint(x, pltpu.VMEM) for x in (one, early, late)))
    return (one[None, None], two[None])


def solution(mesh):
    in_specs = (
        P("row", "col", None, None, None),
        P("row", "col", None),
        P("row", "col", None),
        P("row", "col"),
        P("row", "col", None, None, None),
        P("row", "col", None),
        P("row", "col"),
        P("row", "col", None, None, None),
        P("row", "col", None),
    )
    out_specs = (
        P("row", "col", None, None, None, None, None),
        P("row", None, None, None, None, None),
    )
    return jax.shard_map(
        per_device, mesh=mesh, in_specs=in_specs, out_specs=out_specs, check_vma=False
    )
```

```python
import jax
import jax.numpy as jnp
from jax import lax
from jax.experimental import pallas as pl
from jax.experimental.pallas import tpu as pltpu
from jax.sharding import PartitionSpec as P

BS = 128
FB = 8
CB = 2
NA = 64
NP = 12
G2 = 2
NR = 32
NC = 16
CHIPS = NC // 2
W2 = CB * BS
BF = jnp.bfloat16
F32 = jnp.float32
MESH = pl.DeviceIdType.MESH
VMEM_LIMIT = 67043328 - (1088 << 10)
HALF = (BS, 2 * BS)
REACH = (4, 3, 5, 2, 6, 1, 7)
GROUPS = ((2, 6, 1, 7), (3, 5), (4,))


def dot(a, b):
    return jnp.dot(a, b, preferred_element_type=F32)


def kernel(
    cols_hbm,
    rows_hbm,
    fcount_s,
    codes_hbm,
    pcount_s,
    aggs_hbm,
    a_hbm,
    p_hbm,
    l_hbm,
    one_ref,
    all_e,
    all_l,
    a_buf,
    p_0,
    p_1,
    p_2,
    p_row,
    l_buf,
    meta_v,
    cols_v,
    codes_v,
    aggs_v,
    rows_s,
    table_v,
    table_s,
    near_v,
    near_s,
    pt,
    run,
    wide,
    folded,
    lifted,
    lifted_t,
    give_e,
    give_l,
    take_e,
    take_l,
    part_e,
    part_l,
    rs_e,
    rs_l,
    load_sem,
    halo_send,
    halo_recv,
    pair_send,
    pair_recv,
    rs_send,
    rs_recv,
    ag_send,
    ag_recv,
    fw_send,
    fw_recv,
    reach_sem,
):
    p_bufs = (p_0, p_1, p_2, p_row.at[0], p_row.at[1])
    row = lax.axis_index("row")
    col = lax.axis_index("col")
    chip = col // 2
    core = col % 2
    partner = 2 * chip + 1 - core

    def at(dr, dc):
        return {"row": (row + dr + NR) % NR, "col": (col + dc + NC) % NC}

    sources = ((0, -1), (0, 1), (-1, 0), (1, 0))

    has = (None, col > 0, col < NC - 1, row > 0, row < NR - 1)
    feeds = (None, has[2], has[1], has[4], has[3])

    barrier = pltpu.get_barrier_semaphore()
    for (dr, dc), near in zip(sources, has[1:]):

        @pl.when(near)
        def _():
            pl.semaphore_signal(barrier, inc=1, device_id=at(dr, dc), device_id_type=MESH)


    loads = [
        pltpu.make_async_copy(codes_hbm, codes_v, load_sem.at[0]),
        pltpu.make_async_copy(aggs_hbm, aggs_v, load_sem.at[1]),
        pltpu.make_async_copy(cols_hbm, cols_v, load_sem.at[2]),
        pltpu.make_async_copy(rows_hbm, rows_s, load_sem.at[3]),
        pltpu.make_async_copy(p_hbm, p_0.at[pl.ds(0, NP)], load_sem.at[4]),
        pltpu.make_async_copy(l_hbm, l_buf.at[0], load_sem.at[5]),
        pltpu.make_async_copy(a_hbm, a_buf, load_sem.at[6]),
    ]
    for load in loads:
        load.start()
    for s in range(5):
        p_bufs[s][NP] = jnp.zeros((BS, BS), BF)
    run[NA] = jnp.zeros((W2, BS), F32)

    for s in range(1, 5):

        @pl.when(jnp.logical_not(has[s]))
        def _():
            meta_v[s] = jnp.zeros((8, BS), jnp.int32)
            l_buf[s] = jnp.zeros((CB, BS, BS), BF)

    meta_v[0] = jnp.zeros((8, BS), jnp.int32)
    meta_v[0, 1:2] = jnp.full((1, BS), pcount_s[0, 0], jnp.int32)
    loads[0].wait()
    meta_v[0, 0:1, 0:NP] = codes_v[0]
    loads[1].wait()
    meta_v[0, 2:3, 0:CB] = aggs_v[0]

    pl.semaphore_wait(barrier, sum(near.astype(jnp.int32) for near in has[1:]))

    def halo(s, item):
        src, dst = (
            (meta_v.at[0], meta_v.at[s]),
            (p_0.at[pl.ds(0, NP)], p_bufs[s].at[pl.ds(0, NP)]),
            (l_buf.at[0], l_buf.at[s]),
        )[item]
        dr, dc = sources[s - 1]
        return pltpu.make_async_remote_copy(
            src_ref=src,
            dst_ref=dst,
            send_sem=halo_send.at[s - 1, min(item, 1)],
            recv_sem=halo_recv.at[s - 1, item],
            device_id=at(-dr, -dc),
            device_id_type=MESH,
        )

    loads[4].wait()
    loads[5].wait()
    order = (3, 4, 1, 2)
    for item in range(3):
        for s in order:

            @pl.when(feeds[s])
            def _():
                halo(s, item).start()

    def arrived(s, item):
        @pl.when(has[s])
        def _():
            halo(s, item).wait_recv()


    def spread(step, slot):
        for sign in (-1, 1):

            @pl.when((col + sign * step >= 0) & (col + sign * step < NC))
            def _():
                pl.semaphore_signal(
                    reach_sem.at[slot], inc=1, device_id=at(0, sign * step), device_id_type=MESH
                )

    def known(step, slot):
        ends = (col >= step).astype(jnp.int32) + (col < NC - step).astype(jnp.int32)
        pl.semaphore_wait(reach_sem.at[slot], ends)

    spread(1, 0)

    sub = lax.broadcasted_iota(jnp.int32, (BS, BS), 0)
    lane = lax.broadcasted_iota(jnp.int32, (BS, BS), 1)

    def down(vector, length):
        diag = sub[:length] == lane[:length]
        return jnp.max(jnp.where(diag, vector, -1), axis=1, keepdims=True)

    def pick(match, length, missing):
        best = jnp.max(jnp.where(match, sub[:length], -1), axis=0, keepdims=True)
        return jnp.where(best < 0, missing, best)

    def place(s):
        codes_down = down(meta_v[s, 0:1], 16)
        return pick((codes_down == lane[:16]) & (sub[:16] < meta_v[s, 1:2]), 16, NP)

    loads[2].wait()
    cols = jnp.concatenate([cols_v[0], cols_v[0]], axis=1)
    cols_down = down(cols, NA)
    live = sub[:NA] < fcount_s[0, 0]
    table_v[0:1] = pick((cols_down == cols) & (sub[:NA] < lane[:NA]) & live, NA, NA)
    table_v[1:2] = pick((cols_down == lane[:NA]) & live, NA, NA)
    table_v[2:3] = place(0)
    send_table = pltpu.make_async_copy(table_v, table_s, load_sem.at[7])
    send_table.start()
    for slot in range(NP + 1):
        pt[slot] = p_0[slot].T
    loads[3].wait()
    send_table.wait()
    known(1, 0)
    spread(2, 1)
    loads[6].wait()

    def slots(step, carry):
        for inner in range(4):
            k = step * 4 + inner
            i = rows_s[0, 0, k]
            own = jnp.concatenate([pt[table_s[2, i * CB + j]] for j in range(CB)], axis=0)
            run[k] = dot(own, a_buf[k]) + run[table_s[0, k]]
        return carry

    lax.fori_loop(0, 4, slots, 0)
    known(2, 1)
    spread(4, 2)
    lax.fori_loop(4, 12, slots, 0)
    known(4, 2)
    spread(8, 3)
    for s in range(1, 5):
        arrived(s, 0)
    near_v[0:1] = table_v[2:3]
    near_v[8:9] = meta_v[0, 2:3]
    for s in range(1, 5):
        near_v[s : s + 1] = place(s)
        near_v[8 + s : 9 + s] = meta_v[s, 2:3]
    send_near = pltpu.make_async_copy(near_v, near_s, load_sem.at[8])
    send_near.start()
    lax.fori_loop(12, NA // 4, slots, 0)

    def widen_rows(s, carry):
        for m in range(FB):
            slot = table_s[1, s * FB + m]
            wide[s, m // 2, :, pl.ds((m % 2) * BS, BS)] = run[slot].astype(BF)
        return carry

    lax.fori_loop(0, 5, widen_rows, 0)
    send_near.wait()

    def lift(s):
        for j in range(CB):
            block = l_buf[s, j]
            for a in range(G2):
                kept = jnp.where(near_s[8 + s, j] == a, block, jnp.zeros_like(block))
                lifted[s, pl.ds(j * BS, BS), pl.ds(a * BS, BS)] = kept

    lift(0)
    lifted_t[...] = lifted[0].T

    def dense(block, s, pair):
        return jnp.concatenate(
            [
                jnp.concatenate(
                    [block(near_s[s, (2 * pair + low) * CB + j]) for j in range(CB)], axis=1
                )
                for low in range(2)
            ],
            axis=0,
        )

    def level_one(s):
        total = jnp.zeros((W2, W2), F32)
        for pair in range(FB // 2):
            total += dot(wide[s, pair], dense(lambda slot: p_bufs[s][slot], s, pair))
        result = total.astype(BF)
        for coarse in range(CB):
            for j in range(CB):
                one_ref[coarse, s, j] = result[
                    coarse * BS : (coarse + 1) * BS, j * BS : (j + 1) * BS
                ]
        return result

    def late_half(d):
        total = jnp.zeros((W2, W2), F32)
        for pair in range(FB // 2):
            total += dot(folded[d, pair], dense(lambda slot: p_row[d, slot], 3 + d, pair))
        return total.astype(BF)

    def half_term(firsts):
        total = jnp.zeros((W2, W2), F32)
        for s, result in firsts:
            total += dot(result, lifted[s])
        return dot(lifted_t[...], total.astype(BF))

    takes, parts = (take_e, take_l), (part_e, part_l)
    shares, whole = (rs_e, rs_l), (all_e, all_l)

    def pair_copy(w):
        return pltpu.make_async_remote_copy(
            src_ref=give_l if w else give_e.at[1 - core],
            dst_ref=takes[w],
            send_sem=pair_send.at[w],
            recv_sem=pair_recv.at[w],
            device_id={"row": row, "col": partner},
            device_id_type=MESH,
        )

    def peer(dz):
        return {"row": row, "col": 2 * ((chip + dz) % CHIPS) + core}

    def rs_copy(w, dz):
        return pltpu.make_async_remote_copy(
            src_ref=parts[w].at[(chip + dz) % CHIPS],
            dst_ref=shares[w].at[dz - 1],
            send_sem=rs_send.at[w],
            recv_sem=rs_recv.at[w],
            device_id=peer(dz),
            device_id_type=MESH,
        )

    def together(ref, count, send_sem, recv_sem):
        part = ref.at[pl.ds(0, count)]
        return pltpu.make_async_remote_copy(
            src_ref=part,
            dst_ref=part,
            send_sem=send_sem,
            recv_sem=recv_sem,
            device_id=peer(1),
            device_id_type=MESH,
        )

    def ag_copy(w, dz, group):
        return pltpu.make_async_remote_copy(
            src_ref=whole[w].at[core, chip],
            dst_ref=whole[w].at[core, chip],
            send_sem=ag_send.at[w],
            recv_sem=ag_recv.at[w, group],
            device_id=peer(dz),
            device_id_type=MESH,
        )

    def forward(w, dz):
        piece = whole[w].at[core, (chip - dz + CHIPS) % CHIPS]
        return pltpu.make_async_remote_copy(
            src_ref=piece,
            dst_ref=piece,
            send_sem=fw_send.at[w],
            recv_sem=fw_recv.at[w],
            device_id={"row": row, "col": partner},
            device_id_type=MESH,
        )

    def scatter(w, own):
        pair_copy(w).wait_recv()
        total = own + takes[w][...].astype(F32)
        parts[w][...] = total.astype(BF).reshape(CHIPS, HALF[w] // CHIPS, W2)
        for dz in REACH:
            rs_copy(w, dz).start()

    def gather(w):
        together(shares[w], CHIPS - 1, rs_send.at[w], rs_recv.at[w]).wait_recv()
        total = parts[w][chip].astype(F32)
        for dz in range(1, CHIPS):
            total += shares[w][dz - 1].astype(F32)
        whole[w][core, chip] = total.astype(BF)
        for group in (2, 1, 0):
            for dz in GROUPS[group]:
                ag_copy(w, dz, group).start()
        forward(w, 0).start()

    def hand_over(w, group):
        count = len(GROUPS[group])
        together(whole[w].at[core], count, ag_send.at[w], ag_recv.at[w, group]).wait_recv()
        for dz in GROUPS[group]:
            forward(w, dz).start()

    firsts = [(0, level_one(0))]
    for s in (1, 2):
        arrived(s, 1)
        firsts.append((s, level_one(s)))
    for s in (1, 2):
        arrived(s, 2)
        lift(s)
    early = half_term(firsts).astype(BF)
    for side in range(2):
        give_e[side] = early[side * BS : (side + 1) * BS]
    pair_copy(0).start()
    known(8, 3)
    scatter(0, give_e[core].astype(F32))

    for d in range(2):
        for pair in range(FB // 2):
            folded[d, pair] = dot(lifted_t[...], wide[3 + d, pair]).astype(BF)
    for s in (3, 4):
        arrived(s, 1)
    away, kept = late_half(1 - core), late_half(core)
    for s in (3, 4):
        arrived(s, 2)
        lift(s)
    give_l[...] = dot(away, lifted[4 - core]).astype(BF)
    pair_copy(1).start()
    own = dot(kept, lifted[3 + core])
    scatter(1, own)
    gather(0)
    for s in (3, 4):
        level_one(s)
    gather(1)
    for group in range(3):
        hand_over(0, group)
    for group in range(3):
        hand_over(1, group)
    for s in range(1, 5):

        @pl.when(feeds[s])
        def _():
            halo(s, 0).wait_send()
            together(a_buf, NP + CB, halo_send.at[s - 1, 1], halo_recv.at[s - 1, 1]).wait_send()

    for w in range(2):
        pair_copy(w).wait_send()
        together(parts[w], CHIPS - 1, rs_send.at[w], rs_recv.at[w]).wait_send()
        together(whole[w].at[core], CHIPS - 1, ag_send.at[w], ag_recv.at[w, 0]).wait_send()
        together(whole[w].at[core], CHIPS, fw_send.at[w], fw_recv.at[w]).wait_send()
    for w in range(2):
        together(whole[w].at[1 - core], CHIPS, fw_send.at[w], fw_recv.at[w]).wait_recv()


def finish(one_v, early_v, late_v, one_out, two_out, two_v, give):
    gives = [pltpu.make_async_copy(one_v, one_out, give.at[3])]
    gives[0].start()
    for g in range(3):
        for a in range(G2):
            if g == 0:
                rows = early_v[a].reshape(BS, W2)
            else:
                rows = late_v[g - 1, a * 4 : a * 4 + 4].reshape(BS, W2)
            for b in range(G2):
                two_v[a, g, b] = rows[:, b * BS : (b + 1) * BS].astype(F32)
        gives.append(pltpu.make_async_copy(two_v.at[:, g], two_out.at[:, g], give.at[g]))
        gives[-1].start()
    for copy in gives:
        copy.wait()


def per_device(
    fine_blocks,
    fine_rows,
    fine_cols,
    fine_counts,
    prolong_blocks,
    prolong_codes,
    prolong_counts,
    second_blocks,
    second_aggs,
):
    any_spec = pl.BlockSpec(memory_space=pl.ANY)
    vmem = pl.BlockSpec(memory_space=pltpu.VMEM)
    smem = pl.BlockSpec(memory_space=pltpu.SMEM)
    dma = pltpu.SemaphoreType.DMA
    one, early, late = pl.pallas_call(
        kernel,
        name="galerkin",
        out_shape=(
            pltpu.VMEM((CB, 5, CB, BS, BS), BF),
            pltpu.VMEM((2, CHIPS, HALF[0] // CHIPS, W2), BF),
            pltpu.VMEM((2, CHIPS, HALF[1] // CHIPS, W2), BF),
        ),
        in_specs=[any_spec] * 2 + [smem, any_spec] * 2 + [any_spec] * 3,
        out_specs=(vmem,) * 3,
        scratch_shapes=[
            pltpu.VMEM((NA, BS, BS), BF),
            *[pltpu.VMEM((NP + 1, BS, BS), BF)] * 3,
            pltpu.VMEM((2, NP + 1, BS, BS), BF),
            pltpu.VMEM((5, CB, BS, BS), BF),
            pltpu.VMEM((5, 8, BS), jnp.int32),
            pltpu.VMEM((1, 1, NA), jnp.int32),
            pltpu.VMEM((1, 1, NP), jnp.int32),
            pltpu.VMEM((1, 1, CB), jnp.int32),
            pltpu.SMEM((1, 1, NA), jnp.int32),
            pltpu.VMEM((8, BS), jnp.int32),
            pltpu.SMEM((8, BS), jnp.int32),
            pltpu.VMEM((16, BS), jnp.int32),
            pltpu.SMEM((16, BS), jnp.int32),
            pltpu.VMEM((NP + 1, BS, BS), BF),
            pltpu.VMEM((NA + 1, W2, BS), F32),
            pltpu.VMEM((5, FB // 2, W2, W2), BF),
            pltpu.VMEM((2, FB // 2, W2, W2), BF),
            pltpu.VMEM((5, W2, W2), BF),
            pltpu.VMEM((W2, W2), BF),
            pltpu.VMEM((2, HALF[0], W2), BF),
            pltpu.VMEM((HALF[1], W2), BF),
            pltpu.VMEM((HALF[0], W2), BF),
            pltpu.VMEM((HALF[1], W2), BF),
            pltpu.VMEM((CHIPS, HALF[0] // CHIPS, W2), BF),
            pltpu.VMEM((CHIPS, HALF[1] // CHIPS, W2), BF),
            pltpu.VMEM((CHIPS - 1, HALF[0] // CHIPS, W2), BF),
            pltpu.VMEM((CHIPS - 1, HALF[1] // CHIPS, W2), BF),
            dma((9,)),
            dma((4, 2)),
            dma((4, 3)),
            dma((2,)),
            dma((2,)),
            dma((2,)),
            dma((2,)),
            dma((2,)),
            dma((2, 3)),
            dma((2,)),
            dma((2,)),
            pltpu.SemaphoreType.REGULAR((4,)),
        ],
        compiler_params=pltpu.CompilerParams(
            collective_id=0, has_side_effects=True, vmem_limit_bytes=VMEM_LIMIT
        ),
    )(
        fine_cols,
        fine_rows,
        fine_counts,
        prolong_codes,
        prolong_counts,
        second_aggs,
        fine_blocks[0, 0],
        prolong_blocks[0, 0],
        second_blocks[0, 0],
    )
    one, two = pl.pallas_call(
        finish,
        name="finish",
        out_shape=(
            jax.ShapeDtypeStruct((CB, 5, CB, BS, BS), BF),
            jax.ShapeDtypeStruct((G2, 3, G2, BS, BS), F32),
        ),
        in_specs=[vmem] * 3,
        out_specs=(any_spec,) * 2,
        scratch_shapes=[pltpu.VMEM((G2, 3, G2, BS, BS), F32), dma((4,))],
    )(*(pltpu.with_memory_space_constraint(x, pltpu.VMEM) for x in (one, early, late)))
    return (one[None, None], two[None])


def solution(mesh):
    in_specs = (
        P("row", "col", None, None, None),
        P("row", "col", None),
        P("row", "col", None),
        P("row", "col"),
        P("row", "col", None, None, None),
        P("row", "col", None),
        P("row", "col"),
        P("row", "col", None, None, None),
        P("row", "col", None),
    )
    out_specs = (
        P("row", "col", None, None, None, None, None),
        P("row", None, None, None, None, None),
    )
    return jax.shard_map(
        per_device, mesh=mesh, in_specs=in_specs, out_specs=out_specs, check_vma=False
    )
```
